256 devices in a mesh: segment: 4 (over y), wide: 64 (over z, x, core).
Axes of the slice: x: 4, y: 4, z: 8, core: 2. Of those that a mesh axis runs over, the one named last changes fastest.
Arguments:
- entering_hidden: bfloat16 [2, 128, 8192], P(None, 'wide'), may hold values from -6 to 6
- row_adapter_index: int32 [2, 128, 1], P(None, 'wide'), may hold values from 0 to 63; in each aligned block of 128 rows (0 to 127, 128 to 255, ..., all dimensions but the last counted through in order) at most 4 rows name the same one
- lengths: int32 [2, 128], P(None, 'wide'), may hold values from 2 to 384
- input_norm_gain: bfloat16 [4, 8192], P('segment'), may hold values from 0.099609375 to 1.8984375
- query_matrix: bfloat16 [4, 8192, 8192], P('segment', None, 'wide'), may hold values from -0.0625 to 0.0625
- key_matrix: bfloat16 [4, 8192, 1024], P('segment', None, 'wide'), may hold values from -0.0625 to 0.0625
- value_matrix: bfloat16 [4, 8192, 1024], P('segment', None, 'wide'), may hold values from -0.0625 to 0.0625
- output_matrix: bfloat16 [4, 8192, 8192], P('segment', None, 'wide'), may hold values from -0.0625 to 0.0625
- adapter_down_maps: bfloat16 [4, 64, 8192, 128], P('segment', 'wide'), may hold values from -0.0625 to 0.0625
- adapter_up_query: bfloat16 [4, 64, 64, 8192], P('segment', 'wide'), may hold values from -0.75 to 0.75
- adapter_up_value: bfloat16 [4, 64, 64, 1024], P('segment', 'wide'), may hold values from -0.75 to 0.75
- rotated_key_cache: bfloat16 [4, 2, 128, 384, 1024], P('segment', None, 'wide'), may hold values from -480 to 480
- cached_values: bfloat16 [4, 2, 128, 384, 1024], P('segment', None, 'wide'), may hold values from -6 to 6
Outputs:
- layer_out: bfloat16 [4, 2, 128, 8192], P('segment', None, 'wide')
The draws below stay inside these ranges and needn't reach their ends.
Inputs may be any that keep to these rules, and one draw needn't show every extreme that they name: `row_adapter_index`: in each micro-batch no adapter is named by more than 4 rows.
All inputs are finite; a program needn't handle non-finite values.
Results may differ from the reference program's by a relative error of at most 0.038.
Values may be sent and summed in bfloat16 or wider, within the bound.
A program may use at most 128 MiB of HBM per device.

```python
import math
import jax
import jax.numpy as jnp
import numpy as np
from jax import lax

MODEL_WIDTH = 8192
HEADS = 64
KVH = 8
HD = 128
ADAPTER_RANK = 64
CAP = 4
MICRO = 2
CTX = 384
KEY_FEATURES = 1024
ADAPTER_COUNT = 64
ROWS_MB = 128
N_SEGMENT = 4


def draw_lengths(key, part):
    first, second = jax.random.split(key)
    values = jax.random.randint(first, (MICRO * ROWS_MB,), 2, CTX + 1)
    spot = jax.random.randint(second, (), 0, MICRO * ROWS_MB)
    values = values.at[spot].set(CTX)
    return values.reshape(MICRO, ROWS_MB).astype(jnp.int32)


def draw_rotated_key_cache(key, part):
    first = jax.random.fold_in(key, 0)
    array_shape = (N_SEGMENT, MICRO, ROWS_MB, CTX, KEY_FEATURES)
    entries = jax.random.truncated_normal(first, -6.0, 6.0, array_shape, jnp.float32)
    return entries.astype(jnp.bfloat16)


def shard_levels(own_key, dims, pieces, low, top_value):
    def one(dim, blocks):
        steps = jax.random.uniform(jax.random.fold_in(jax.random.fold_in(own_key, 6), dim), (blocks,), jnp.float32, low / len(pieces), top_value / len(pieces))
        return jnp.repeat(jnp.exp(steps), dims[dim] // blocks).reshape((-1,) + (1,) * (len(dims) - dim - 1))

    loudness = one(*pieces[0])
    for cut in pieces[1:]:
        loudness = loudness * one(*cut)
    return loudness


def shared_out(stream_key, own, number, rows, number_of, top, bound, lean):
    ranking = jax.random.permutation(stream_key, number_of)
    crowded, ordinary = shares(number_of, rows * top, bound, lean, True), shares(number_of, rows * top, bound, lean, False)
    places = jnp.arange(number_of)

    def named(tallies, turn):
        used = int((tallies > 0).sum())
        fixed = max(1, used // 4)
        shifted = fixed + (places - fixed + turn * (used - fixed)) % max(1, number_of - fixed)
        return jnp.zeros((number_of,), jnp.int32).at[ranking[jnp.where(places < fixed, places, shifted)]].set(jnp.asarray(tallies, jnp.int32))

    tallies = jnp.where(number % 4 == 0, named(crowded, number // 4), named(ordinary, number - number // 4 - 1))
    mixed = jax.random.permutation(jax.random.fold_in(own, 3), number_of)
    donor, receiver = mixed[0:number_of // 2 * 2:2], mixed[1:number_of // 2 * 2:2]
    room = jnp.minimum(tallies[donor] - 1, bound - tallies[receiver]) // 2
    room = jnp.where((donor == ranking[0]) | (receiver == ranking[0]) | (tallies[receiver] == 0), 0, jnp.maximum(room, 0))
    shifted = jax.random.randint(jax.random.fold_in(own, 4), (number_of // 2,), 0, 1 << 20) % (room + 1)
    tallies = tallies.at[donor].add(-shifted).at[receiver].add(shifted)
    members = jnp.searchsorted(jnp.cumsum(tallies), jnp.arange(rows * top), side="right").astype(jnp.int32)
    listing = members.reshape(top, rows).T
    listing = listing[jax.random.permutation(jax.random.fold_in(own, 1), rows)]
    turn = jax.random.randint(jax.random.fold_in(own, 2), (rows, 1), 0, top)
    return jnp.take_along_axis(listing, (jnp.arange(top)[None, :] + turn) % top, axis=1)


def shares(amount, total, bound, slope, full):
    loads = [(1 << 20) // math.isqrt(standing ** slope) + 1 for standing in range(1, amount + 1)]
    largest = bound if full else min(bound, max(-(-total // amount), total * loads[0] // sum(loads)))
    least = 1 if total - largest >= amount - 1 else 0
    holding, spare = [largest] + [least] * (amount - 1), total - largest - least * (amount - 1)
    while spare > 0:
        free = [i for i in range(1, amount) if holding[i] < largest] or [i for i in range(1, amount) if holding[i] < bound]
        mass, left = sum([loads[i] for i in free]), spare
        for i in free:
            extra = min(bound - holding[i], max(1, left * loads[i] // mass), spare)
            holding[i] = holding[i] + extra
            spare = spare - extra
    return np.array(holding)


def scatter_about(key, extent, width, most, cuts=(), kind=jnp.bfloat16):
    level = shard_levels(key, extent, cuts, -0.22, 0.18) if cuts else 1.0
    drawn = jax.random.normal(key, extent, jnp.float32) * width * level
    return jnp.minimum(jnp.maximum(drawn, -most), most).astype(kind)


def setup_inputs(seed: int = 0) -> dict:
    splits = jax.random.split(jax.random.key(seed), 14)
    entering_hidden = scatter_about(splits[0], (MICRO, ROWS_MB, MODEL_WIDTH), 1.0, 6.0, ((1, 64),))
    row_adapter_index_keys = jax.random.split(jax.random.fold_in(splits[1], 1), MICRO * ROWS_MB // ROWS_MB)
    row_adapter_index_turns = jax.random.permutation(jax.random.fold_in(splits[1], 3), MICRO * ROWS_MB // ROWS_MB)
    row_adapter_index = jax.vmap(lambda own, number: shared_out(jax.random.fold_in(splits[1], 2), own, number, ROWS_MB, ADAPTER_COUNT, 1, CAP, 2))(row_adapter_index_keys, row_adapter_index_turns).reshape((MICRO, ROWS_MB, 1))
    lengths = draw_lengths(jax.random.fold_in(splits[13], 71), 0)
    input_norm_gain = jnp.clip(1.0 + 0.18 * jax.random.normal(splits[3], (N_SEGMENT, MODEL_WIDTH), jnp.float32), 0.099609375, 1.8984375).astype(jnp.bfloat16)
    query_matrix = scatter_about(splits[4], (N_SEGMENT, MODEL_WIDTH, MODEL_WIDTH), MODEL_WIDTH ** -0.5, 0.0625, ((0, 4), (2, 64)))
    key_matrix = scatter_about(splits[5], (N_SEGMENT, MODEL_WIDTH, KEY_FEATURES), MODEL_WIDTH ** -0.5, 0.0625, ((0, 4), (2, 64)))
    value_matrix = scatter_about(splits[6], (N_SEGMENT, MODEL_WIDTH, KEY_FEATURES), MODEL_WIDTH ** -0.5, 0.0625, ((0, 4), (2, 64)))
    output_matrix = scatter_about(splits[7], (N_SEGMENT, MODEL_WIDTH, MODEL_WIDTH), MODEL_WIDTH ** -0.5, 0.0625, ((0, 4), (2, 64)))
    adapter_down_maps = scatter_about(splits[8], (N_SEGMENT, ADAPTER_COUNT, MODEL_WIDTH, 2 * ADAPTER_RANK), MODEL_WIDTH ** -0.5, 0.0625, ((0, 4), (1, 64)))
    adapter_up_query = scatter_about(splits[9], (N_SEGMENT, ADAPTER_COUNT, ADAPTER_RANK, MODEL_WIDTH), ADAPTER_RANK ** -0.5, 0.75, ((0, 4), (1, 64)))
    adapter_up_value = scatter_about(splits[10], (N_SEGMENT, ADAPTER_COUNT, ADAPTER_RANK, KEY_FEATURES), ADAPTER_RANK ** -0.5, 0.75, ((0, 4), (1, 64)))
    rotated_key_cache = draw_rotated_key_cache(jax.random.fold_in(splits[13], 71), 0)
    cached_values = scatter_about(splits[12], (N_SEGMENT, MICRO, ROWS_MB, CTX, KEY_FEATURES), 1.0, 6.0, ((0, 4), (2, 64)))
    return {"entering_hidden": entering_hidden, "row_adapter_index": row_adapter_index, "lengths": lengths, "input_norm_gain": input_norm_gain, "query_matrix": query_matrix, "key_matrix": key_matrix, "value_matrix": value_matrix, "output_matrix": output_matrix, "adapter_down_maps": adapter_down_maps, "adapter_up_query": adapter_up_query, "adapter_up_value": adapter_up_value, "rotated_key_cache": rotated_key_cache, "cached_values": cached_values}


adapter_scale = 0.5
rope_base = 500000.0
epsilon = 1e-05

def rotary(vectors, positions):
    half = vectors.shape[-1] // 2
    inverse = rope_base ** (-jnp.arange(half, dtype=jnp.float32) / half)
    angles = positions.astype(jnp.float32)[:, None] * inverse[None, :]
    cosine = jnp.cos(angles)[:, None, :]
    sine = jnp.sin(angles)[:, None, :]
    front = vectors[..., :half]
    back = vectors[..., half:]
    return jnp.concatenate([front * cosine - back * sine, back * cosine + front * sine], -1)

def adapter_deltas(normalized_rows, idents, down, up_query, up_value):

    def one_row(inputs):
        row, ident = inputs
        low = jnp.dot(row, down[ident], preferred_element_type=jnp.float32).astype(jnp.bfloat16)
        query_adjustment = jnp.dot(low[:ADAPTER_RANK], up_query[ident], preferred_element_type=jnp.float32)
        value_adjustment = jnp.dot(low[ADAPTER_RANK:], up_value[ident], preferred_element_type=jnp.float32)
        return (query_adjustment, value_adjustment)
    return lax.map(one_row, (normalized_rows, idents))

def apply_layer(hidden_rows, idents, positions, gain, query_matrix, key_matrix, value_matrix, output_matrix, down, up_query, up_value, key_block, value_block):
    rows = hidden_rows.shape[0]
    values = hidden_rows.astype(jnp.float32)
    normalized_rows = (values * lax.rsqrt(lax.optimization_barrier(jnp.mean(values * values, 1, keepdims=True)) + epsilon) * gain.astype(jnp.float32)).astype(jnp.bfloat16)
    query_adjustment, value_adjustment = adapter_deltas(normalized_rows, idents, down, up_query, up_value)
    query_vector = (jnp.dot(normalized_rows, query_matrix, preferred_element_type=jnp.float32) + adapter_scale * query_adjustment).astype(jnp.bfloat16)
    new_key = jnp.dot(normalized_rows, key_matrix, preferred_element_type=jnp.float32).astype(jnp.bfloat16)
    fresh_value = (jnp.dot(normalized_rows, value_matrix, preferred_element_type=jnp.float32) + adapter_scale * value_adjustment).astype(jnp.bfloat16)
    group = HEADS // KVH
    rotated_rows = rotary(query_vector.astype(jnp.float32).reshape(rows, HEADS, HD), positions).astype(jnp.bfloat16)
    rotated_rows = rotated_rows.reshape(rows, KVH, group, HD).astype(jnp.float32)
    self_key = rotary(new_key.astype(jnp.float32).reshape(rows, KVH, HD), positions).astype(jnp.bfloat16).astype(jnp.float32)
    keys_past = key_block.reshape(rows, CTX, KVH, HD).astype(jnp.float32)
    values_past = value_block.reshape(rows, CTX, KVH, HD).astype(jnp.float32)
    score_scale = HD ** (-0.5)
    past = jnp.einsum('bkgd,bpkd->bkgp', rotated_rows, keys_past) * score_scale
    self_scores = jnp.einsum('rice,rie->ric', rotated_rows, self_key) * score_scale
    valid = jnp.arange(CTX)[None, :] < positions[:, None]
    past = jnp.where(valid[:, None, None, :], past, -1e+30)
    top = jnp.maximum(lax.optimization_barrier(jnp.max(past, -1)), self_scores)
    past_exp = jnp.where(valid[:, None, None, :], jnp.exp(past - top[..., None]), 0.0)
    own_exp = jnp.exp(self_scores - top)
    total = lax.optimization_barrier(jnp.sum(past_exp, -1)) + own_exp
    past_weights = (past_exp / total[..., None]).astype(jnp.bfloat16).astype(jnp.float32)
    own_weights = (own_exp / total).astype(jnp.bfloat16).astype(jnp.float32)
    mixed = jnp.einsum('bkgp,bpkd->bkgd', past_weights, values_past)
    mixed = mixed + own_weights[..., None] * fresh_value.reshape(rows, KVH, HD).astype(jnp.float32)[:, :, None, :]
    attended = mixed.reshape(rows, HEADS * HD).astype(jnp.bfloat16)
    projected = jnp.dot(attended, output_matrix, preferred_element_type=jnp.float32)
    return (values + projected).astype(jnp.bfloat16)

def reference(entering_hidden, row_adapter_index, lengths, input_norm_gain, query_matrix, key_matrix, value_matrix, output_matrix, adapter_down_maps, adapter_up_query, adapter_up_value, rotated_key_cache, cached_values):
    per_layer = [[None] * MICRO for layer_number in range(N_SEGMENT)]
    for small_batch in range(MICRO):
        hidden_rows = entering_hidden[small_batch]
        for layer_number in range(N_SEGMENT):
            hidden_rows = apply_layer(hidden_rows, row_adapter_index[small_batch, :, 0], lengths[small_batch], input_norm_gain[layer_number], query_matrix[layer_number], key_matrix[layer_number], value_matrix[layer_number], output_matrix[layer_number], adapter_down_maps[layer_number], adapter_up_query[layer_number], adapter_up_value[layer_number], rotated_key_cache[layer_number, small_batch], cached_values[layer_number, small_batch])
            per_layer[layer_number][small_batch] = hidden_rows
    return jnp.stack([jnp.stack(per_layer[layer_number]) for layer_number in range(N_SEGMENT)])
```

```python
import jax
import jax.numpy as jnp
from jax import lax
from jax.experimental import pallas as pl
from jax.experimental.pallas import tpu as pltpu
from jax.sharding import PartitionSpec as P

HD = 128
RANK = 64
EPS = 1e-05
ROPE_BASE = 500000.0
ZS, XS, CS = 8, 4, 2
MESH = pl.DeviceIdType.MESH
F32 = jnp.float32
BF16 = jnp.bfloat16


def iota(shape, dim):
    return lax.broadcasted_iota(jnp.int32, shape, dim)


def onehot(cond):
    return jnp.where(cond, 1.0, 0.0).astype(BF16)


def dot(a, b):
    return jnp.dot(a, b, preferred_element_type=F32)


def dot_nt(a, b):
    return lax.dot_general(a, b, (((1,), (1,)), ((), ())), preferred_element_type=F32)


def kernel(
    h0_ref, aux_ref, gain_ref, wq_hbm, wk_hbm, wv_hbm, wo_hbm, down_hbm, upq_hbm, upv_hbm, kc_hbm, vc_hbm,
    out_ref,
    wq, wkv, wo, down, upq, upv, kc, vc,
    hst, tmp, hin, hout,
    xb1, xb2, xg, ag, acc_q, acc_kv, acc_d,
    ix_send, ix_mid, ix_recv, co_send, co_mid, co_recv, qk_send, qk_mid, qk_recv, ou_send, ou_mid, ou_recv,
    tq, tv, chosen,
    wsem, xsem_s, xsem_r, zsem_s, zsem_r, psem_s, psem_r, asem_s, asem_r, hsem,
):
    seg = lax.axis_index("segment")
    me = lax.axis_index("wide")
    nseg = lax.axis_size("segment")
    z = me // (XS * CS)
    xc = me % (XS * CS)
    x = xc // CS
    c = xc % CS
    grp = z * CS + c

    def wide(zz, xx, cc):
        return {"wide": (zz * XS + xx) * CS + cc}

    def remote(src, dst, ssem, rsem, dev):
        return pltpu.make_async_remote_copy(
            src_ref=src, dst_ref=dst, send_sem=ssem, recv_sem=rsem, device_id=dev, device_id_type=MESH
        )

    loads = [
        pltpu.make_async_copy(wq_hbm, wq, wsem.at[0]),
        pltpu.make_async_copy(wk_hbm, wkv.at[pl.ds(0, 16)], wsem.at[1]),
        pltpu.make_async_copy(wv_hbm, wkv.at[pl.ds(16, 16)], wsem.at[2]),
        pltpu.make_async_copy(down_hbm, down, wsem.at[3]),
        pltpu.make_async_copy(upq_hbm, upq.at[pl.ds(0, RANK)], wsem.at[4]),
        pltpu.make_async_copy(upv_hbm, upv.at[pl.ds(RANK, RANK)], wsem.at[5]),
        pltpu.make_async_copy(kc_hbm, kc, wsem.at[6]),
        pltpu.make_async_copy(vc_hbm, vc, wsem.at[7]),
        pltpu.make_async_copy(wo_hbm, wo, wsem.at[8]),
    ]
    for load in loads:
        load.start()

    barrier = pltpu.get_barrier_semaphore()
    for k in range(1, 8):
        other = (xc + k) % 8
        pl.semaphore_signal(barrier, inc=1, device_id={"wide": z * 8 + other}, device_id_type=MESH)
        pl.semaphore_signal(barrier, inc=1, device_id={"wide": ((z + k) % 8) * 8 + xc}, device_id_type=MESH)

    for k in (1, nseg - 1):
        pl.semaphore_signal(barrier, inc=1, device_id={"segment": (seg + k) % nseg}, device_id_type=MESH)
    pl.semaphore_wait(barrier, 16)

    pending = []

    def exchange(number, send, mid, recv, rows):
        first = pltpu.make_async_copy(send.at[xc], mid.at[:, pl.ds(pl.multiple_of(xc * rows, rows), rows), :], asem_r.at[number, 0])
        first.start()
        for k in range(1, 8):
            other = (xc + k) % 8
            remote(
                send.at[other], mid.at[:, pl.ds(pl.multiple_of(xc * rows, rows), rows), :],
                asem_s.at[number, 0], asem_r.at[number, 0], {"wide": z * 8 + other},
            ).start()
        pltpu.make_async_copy(mid, mid, asem_r.at[number, 0]).wait()
        mine = pl.ds(pl.multiple_of(z * 8 * rows, 8 * rows), 8 * rows)
        pltpu.make_async_copy(mid.at[z], recv.at[mine], asem_r.at[number, 1]).start()
        for k in range(1, 8):
            other = (z + k) % 8
            remote(
                mid.at[other], recv.at[mine], asem_s.at[number, 1], asem_r.at[number, 1], {"wide": other * 8 + xc}
            ).start()

    def arrived(number, send, mid, recv):
        pltpu.make_async_copy(recv, recv, asem_r.at[number, 1]).wait()
        pending.append(lambda: pltpu.make_async_copy(send.at[pl.ds(0, 7)], send.at[pl.ds(0, 7)], asem_s.at[number, 0]).wait())
        pending.append(lambda: pltpu.make_async_copy(mid.at[pl.ds(0, 7)], mid.at[pl.ds(0, 7)], asem_s.at[number, 1]).wait())

    def gather(number, xb, full):
        base = pl.multiple_of(x * 16, 16)
        for m in range(16):
            xb[pl.ds(base, 16), m * 128:(m + 1) * 128] = tmp[pl.ds(m, 16, stride=16), :].astype(BF16)
        hops = []
        for k in range(1, XS):
            own = xb.at[pl.ds(base, 16)]
            hop = remote(own, own, xsem_s.at[number, k - 1], xsem_r.at[number, k - 1], wide(z, (x + k) % XS, c))
            hop.start()
            hops.append(hop)
        for hop in hops:
            hop.wait_recv()
            pending.append(hop.wait_send)
        i, k = iota((64, 64), 0), iota((64, 64), 1)
        perm = onehot(k == ((i >> 2) & 3) * 16 + (i & 3) * 4 + (i >> 4))
        own_rows = pl.ds(pl.multiple_of(grp * 16, 16), 16)
        for part in range(4):
            moved = dot(perm, xb[:, part * 512:(part + 1) * 512]).astype(BF16)
            for q in range(4):
                full[own_rows, q * 2048 + part * 512:q * 2048 + (part + 1) * 512] = moved[16 * q:16 * q + 16]

        def piece(offset, half, core):
            at = pl.multiple_of((((z + offset) % ZS) * CS + core) * 16, 16)
            return full.at[pl.ds(at, 16), pl.ds(half * 4096, 4096)]

        def ring(direction, step, half):
            offset = (-step if direction == 0 else step) + ZS
            block = piece(offset, half, c)
            target = (z + (1 if direction == 0 else ZS - 1)) % ZS
            return remote(block, block, zsem_s.at[number, direction, step, half], zsem_r.at[number, direction, step, half], wide(target, x, c))

        def landed(direction, step, half):
            offset = (-(step + 1) if direction == 0 else step + 1) + ZS
            block = piece(offset, half, c)
            remote(block, block, zsem_s.at[number, direction, step, half], zsem_r.at[number, direction, step, half], wide(z, x, 1 - c)).wait_recv()

        def share(offset, half):
            offset = offset % ZS
            block = piece(offset, half, c)
            copy = remote(block, block, psem_s.at[number, offset, half], psem_r.at[number, offset, half], wide(z, x, 1 - c))
            copy.start()
            pending.append(copy.wait_send)

        for half in range(2):
            for direction in range(2):
                copy = ring(direction, 0, half)
                copy.start()
                pending.append(copy.wait_send)
        for half in range(2):
            share(0, half)
        for step in range(3):
            for half in range(2):
                for direction in range(2):
                    landed(direction, step, half)
                    if step < 2 or half == direction:
                        copy = ring(direction, step + 1, half)
                        copy.start()
                        pending.append(copy.wait_send)
                    share(-(step + 1) if direction == 0 else step + 1, half)
        for direction in range(2):
            landed(direction, 3, direction)
            share(4, direction)
        for offset in range(ZS):
            for half in range(2):
                block = piece(offset, half, 1 - c)
                remote(block, block, psem_s.at[number, offset, half], psem_r.at[number, offset, half], wide(z, x, 1 - c)).wait_recv()

    ix = jnp.broadcast_to(aux_ref[16:24, :][None], (8, 8, 128))
    for i in range(8):
        ix_send[i] = ix
    exchange(0, ix_send, ix_mid, ix_recv, 8)

    wkv[32:128, :] = jnp.zeros((96, wkv.shape[1]), BF16)
    upq[RANK:2 * RANK, :] = jnp.zeros((RANK, upq.shape[1]), BF16)
    upv[0:RANK, :] = jnp.zeros((RANK, upv.shape[1]), BF16)

    arrived(0, ix_send, ix_mid, ix_recv)
    i, k = iota((256, 512), 0), iota((256, 512), 1)
    source = (((i >> 5) * XS + ((i >> 2) & 3)) * CS + ((i >> 4) & 1)) * 8 + (i & 3)
    column = dot(onehot(k == source), ix_recv[...].astype(BF16))
    row = column.T
    same = jnp.broadcast_to(column[:, 0:1], (256, 256)) == jnp.broadcast_to(row[0:1, :], (256, 256))
    before = same & (iota((256, 256), 1) < iota((256, 256), 0))
    order = jnp.sum(jnp.where(before, 1.0, 0.0), axis=1, keepdims=True)
    slot = (column[:, 0:1] * 16.0 + order).astype(jnp.int32)
    spots = iota((256, 1024), 1)
    tq[...] = onehot(spots == slot)
    tv[...] = onehot(spots == slot + 8)
    order_row = jnp.broadcast_to(order, (256, 128)).T
    mine = (row[0:16, :].astype(jnp.int32) == me) & (order_row[0:16, :].astype(jnp.int32) == iota((16, 256), 0))
    chosen[...] = onehot(mine)

    @pl.when(seg == 0)
    def _():
        hst[...] = h0_ref[...].astype(F32)

    @pl.when(seg > 0)
    def _():
        remote(hout, hin, hsem.at[0], hsem.at[1], {"segment": seg - 1}).wait_recv()
        hst[...] = hin[...].astype(F32)

    gain = gain_ref[...]
    for r in range(4):
        block = hst[r * 64:(r + 1) * 64, :]
        total = jnp.sum(jnp.sum(block * block, axis=1, keepdims=True), axis=0, keepdims=True)
        tmp[r * 64:(r + 1) * 64, :] = block * lax.rsqrt(total * (1.0 / 8192.0) + EPS) * gain

    gather(0, xb1, xg)

    for n in range(6):
        loads[n].wait()
    acc_q[...] = jnp.zeros_like(acc_q)
    acc_kv[...] = jnp.zeros_like(acc_kv)
    acc_d[...] = jnp.zeros_like(acc_d)

    @pl.loop(0, 8)
    def _(n):
        part = pl.ds(pl.multiple_of(n * 1024, 1024), 1024)
        block = xg[:, part]
        acc_d[...] += dot(block, down[part, :])
        acc_q[...] += dot(block, wq[part, :])
        acc_kv[...] += dot_nt(block, wkv[:, part])

    low = dot(chosen[...], acc_d[...].astype(BF16)).astype(BF16)
    for part in range(8):
        q_slots = dot(low, upq[:, part * 1024:(part + 1) * 1024])
        v_slots = dot(low, upv[:, part * 128:(part + 1) * 128])
        for n in range(8):
            tile = jnp.concatenate([q_slots[0:8, n * 128:(n + 1) * 128], v_slots[0:8, :]], axis=0)
            co_send[n, part] = tile.astype(BF16)
    exchange(1, co_send, co_mid, co_recv, 16)
    arrived(1, co_send, co_mid, co_recv)

    a, b = iota((128, 128), 0), iota((128, 128), 1)
    moved = co_recv[...]
    query = acc_q[...] + 0.5 * dot(tq[...], moved)
    mine = onehot((b >= 16) & (b < 32) & (a == (xc * 16 - 16) + b))
    fresh = acc_kv[...] + 0.5 * dot(dot(tv[...], moved).astype(BF16), mine)
    query = query.astype(BF16).astype(F32).reshape(32, 8, 128)
    fresh = fresh.astype(BF16).astype(F32).reshape(32, 8, 128)
    upper = iota((32, 8, 128), 1) < 4
    even = jnp.where(upper, query, pltpu.roll(fresh, 4, 1))
    odd = jnp.where(upper, pltpu.roll(query, 4, 1), fresh)
    for p in range(64):
        qk_send[(p % 4) * 2 + (p // 4) % 2, p // 8] = (even if p % 2 == 0 else odd)[p // 2]
    exchange(2, qk_send, qk_mid, qk_recv, 8)
    arrived(2, qk_send, qk_mid, qk_recv)

    loads[6].wait()
    loads[7].wait()
    spread_k = onehot(a == (b & 15))
    spread_v = onehot(a == (b & 15) + 16)
    a, b = iota((64, 128), 0), iota((64, 128), 1)
    lanes = (b >> 4) == (a & 7)
    a, b = iota((64, 64), 0), iota((64, 64), 1)
    heads = onehot((a >> 3) == (b >> 3))
    a, b = iota((64, 1024), 0), iota((64, 1024), 1)
    diagonal = (b >> 7) == (a >> 3)
    past = iota((64, 384), 1)
    scale = HD ** (-0.5)
    for r in range(4):
        cosine, sine = aux_ref[r:r + 1, :], aux_ref[4 + r:5 + r, :]
        length = aux_ref[8 + r:9 + r, 0:1].astype(jnp.int32)
        q_row = qk_recv[pl.ds(r, 64, stride=8), :]
        kv_row = qk_recv[pl.ds(4 + r, 64, stride=8), :].astype(BF16)
        k_row = dot(heads, jnp.where(lanes, dot(kv_row, spread_k), 0.0).astype(BF16))
        v_row = dot(heads, jnp.where(lanes, dot(kv_row, spread_v), 0.0).astype(BF16))
        q_rot = (q_row * cosine + pltpu.roll(q_row, 64, 1) * sine).astype(BF16).astype(F32)
        k_rot = (k_row * cosine + pltpu.roll(k_row, 64, 1) * sine).astype(BF16).astype(F32)
        own = jnp.sum(q_rot * k_rot, axis=1, keepdims=True) * scale
        wide_q = jnp.where(diagonal, jnp.concatenate([q_rot] * 8, axis=1), 0.0).astype(BF16)
        scores = dot_nt(wide_q, kc[r * 384:(r + 1) * 384, :]) * scale
        valid = past < length
        scores = jnp.where(valid, scores, -1e30)
        top = jnp.maximum(jnp.max(scores, axis=1, keepdims=True), own)
        powers = jnp.where(valid, jnp.exp(scores - top), 0.0)
        own_power = jnp.exp(own - top)
        total = jnp.sum(powers, axis=1, keepdims=True) + own_power
        weights = (powers / total).astype(BF16)
        own_weight = (own_power / total).astype(BF16).astype(F32)
        mixed = dot(weights, vc[r * 384:(r + 1) * 384, :])
        mixed = jnp.concatenate([mixed[8 * g:8 * g + 8, 128 * g:128 * g + 128] for g in range(8)], axis=0)
        tmp[r * 64:(r + 1) * 64, :] = mixed + own_weight * v_row

    gather(1, xb2, ag)

    loads[8].wait()
    acc_q[...] = jnp.zeros_like(acc_q)

    @pl.loop(0, 8)
    def _(n):
        part = pl.ds(pl.multiple_of(n * 1024, 1024), 1024)
        acc_q[...] += dot(ag[:, part], wo[part, :])

    even = acc_q[...].reshape(32, 8, 128)
    odd = pltpu.roll(even, 4, 1)
    for p in range(64):
        ou_send[(p % 4) * 2 + (p // 4) % 2, p // 8] = (even if p % 2 == 0 else odd)[p // 2]
    exchange(3, ou_send, ou_mid, ou_recv, 8)
    arrived(3, ou_send, ou_mid, ou_recv)
    for r in range(4):
        rows = slice(r * 64, (r + 1) * 64)
        result = (hst[rows, :] + ou_recv[pl.ds(r, 64, stride=8), :]).astype(BF16)
        out_ref[rows, :] = result
        hout[rows, :] = result

    @pl.when(seg < nseg - 1)
    def _():
        passing = remote(hout, hin, hsem.at[0], hsem.at[1], {"segment": seg + 1})
        passing.start()
        passing.wait_send()

    for wait in pending:
        wait()


def on_device(
    entering_hidden, row_adapter_index, lengths, input_norm_gain, query_matrix, key_matrix, value_matrix,
    output_matrix, adapter_down_maps, adapter_up_query, adapter_up_value, rotated_key_cache, cached_values,
):
    half = HD // 2
    positions = lengths.reshape(4, 1).astype(F32)
    inverse = ROPE_BASE ** (-jnp.arange(half, dtype=F32) / half)
    angles = positions * inverse[None, :]
    cosine, sine = jnp.cos(angles), jnp.sin(angles)
    spread = lambda v: jnp.pad(jnp.broadcast_to(v, (4, 128)), ((0, 4), (0, 0)))
    aux = jnp.concatenate(
        [
            jnp.concatenate([cosine, cosine], 1),
            jnp.concatenate([-sine, sine], 1),
            spread(positions),
            spread(row_adapter_index.reshape(4, 1).astype(F32)),
        ],
        0,
    )
    vmem = pl.BlockSpec(memory_space=pltpu.VMEM)
    hbm = pl.BlockSpec(memory_space=pl.ANY)
    tiles = lambda rows, kind: [
        pltpu.VMEM((8, 8, rows, 128), kind), pltpu.VMEM((8, 8 * rows, 128), kind), pltpu.VMEM((64 * rows, 128), kind)
    ]
    dma = pltpu.SemaphoreType.DMA
    out = pl.pallas_call(
        kernel,
        out_shape=jax.ShapeDtypeStruct((256, 128), BF16),
        in_specs=[vmem] * 3 + [hbm] * 9,
        out_specs=vmem,
        scratch_shapes=[
            pltpu.VMEM((8192, 128), BF16), pltpu.VMEM((128, 8192), BF16), pltpu.VMEM((8192, 128), BF16),
            pltpu.VMEM((8192, 128), BF16), pltpu.VMEM((128, 8192), BF16), pltpu.VMEM((128, 1024), BF16),
            pltpu.VMEM((1536, 1024), BF16), pltpu.VMEM((1536, 1024), BF16),
            pltpu.VMEM((256, 128), F32), pltpu.VMEM((256, 128), F32),
            pltpu.VMEM((256, 128), BF16), pltpu.VMEM((256, 128), BF16),
            pltpu.VMEM((64, 2048), BF16), pltpu.VMEM((64, 2048), BF16),
            pltpu.VMEM((256, 8192), BF16), pltpu.VMEM((256, 8192), BF16),
            pltpu.VMEM((256, 128), F32), pltpu.VMEM((256, 128), F32), pltpu.VMEM((256, 128), F32),
            *tiles(8, F32), *tiles(16, BF16), *tiles(8, F32), *tiles(8, F32),
            pltpu.VMEM((256, 1024), BF16), pltpu.VMEM((256, 1024), BF16), pltpu.VMEM((16, 256), BF16),
            dma((9,)), dma((2, 3)), dma((2, 3)), dma((2, 2, 4, 2)), dma((2, 2, 4, 2)),
            dma((2, 8, 2)), dma((2, 8, 2)), dma((4, 2)), dma((4, 2)), dma((2,)),
        ],
        compiler_params=pltpu.CompilerParams(
            collective_id=0, has_side_effects=True, vmem_limit_bytes=60 * 1024 * 1024
        ),
        name="layer_step",
    )(
        entering_hidden.reshape(256, 128),
        aux,
        input_norm_gain.astype(F32).reshape(64, 128),
        query_matrix[0],
        key_matrix[0].T,
        value_matrix[0].T,
        output_matrix[0],
        adapter_down_maps[0, 0],
        adapter_up_query[0, 0],
        adapter_up_value[0, 0],
        rotated_key_cache.reshape(1536, 1024),
        cached_values.reshape(1536, 1024),
    )
    return out.reshape(1, 2, 2, 8192)


def solution(mesh):
    placed = (
        P(None, "wide", None), P(None, "wide", None), P(None, "wide"), P("segment", None),
        P("segment", None, "wide"), P("segment", None, "wide"), P("segment", None, "wide"), P("segment", None, "wide"),
        P("segment", "wide", None, None), P("segment", "wide", None, None), P("segment", "wide", None, None),
        P("segment", None, "wide", None, None), P("segment", None, "wide", None, None),
    )
    return jax.shard_map(
        on_device, mesh=mesh, in_specs=placed, out_specs=P("segment", None, "wide", None), check_vma=False
    )
```

```python
import jax
import jax.numpy as jnp
from jax import lax
from jax.experimental import pallas as pl
from jax.experimental.pallas import tpu as pltpu
from jax.sharding import PartitionSpec as P

HD = 128
RANK = 64
EPS = 1e-05
ROPE_BASE = 500000.0
ZS, XS, CS = 8, 4, 2
MESH = pl.DeviceIdType.MESH
F32 = jnp.float32
BF16 = jnp.bfloat16


def iota(shape, dim):
    return lax.broadcasted_iota(jnp.int32, shape, dim)


def onehot(cond):
    return jnp.where(cond, 1.0, 0.0).astype(BF16)


def dot(a, b):
    return jnp.dot(a, b, preferred_element_type=F32)


def dot_nt(a, b):
    return lax.dot_general(a, b, (((1,), (1,)), ((), ())), preferred_element_type=F32)


def kernel(
    h0_ref, aux_ref, gain_ref, wq_hbm, wk_hbm, wv_hbm, wo_hbm, down_hbm, upq_hbm, upv_hbm, kc_hbm, vc_hbm,
    out_ref,
    wq, wkv, wo, down, upq, upv, kc, vc,
    hst, tmp, hin, hout,
    xb1, xb2, fb1, fb2, xg, ag, acc_q, acc_kv, acc_d,
    ix_send, ix_mid, ix_recv, co_send, co_mid, co_recv, qk_send, qk_mid, qk_swap, qk_recv, ou_send, ou_mid, ou_swap, ou_recv,
    tq, tv, chosen, perm_a, perm_b, perm_c, rows_q,
    wsem, xa_s, xa_r, za_s, za_r, ua_s, ua_r, zb_s, zb_r, xb_s, xb_r, ub_s, ub_r, asem_s, asem_r, hsem,
):
    seg = lax.axis_index("segment")
    me = lax.axis_index("wide")
    nseg = lax.axis_size("segment")
    z = me // (XS * CS)
    xc = me % (XS * CS)
    x = xc // CS
    c = xc % CS
    grp = z * CS + c

    def wide(zz, xx, cc):
        return {"wide": (zz * XS + xx) * CS + cc}

    def remote(src, dst, ssem, rsem, dev):
        return pltpu.make_async_remote_copy(
            src_ref=src, dst_ref=dst, send_sem=ssem, recv_sem=rsem, device_id=dev, device_id_type=MESH
        )

    loads = [
        pltpu.make_async_copy(wq_hbm, wq, wsem.at[0]),
        pltpu.make_async_copy(wk_hbm, wkv.at[pl.ds(0, 16)], wsem.at[1]),
        pltpu.make_async_copy(wv_hbm, wkv.at[pl.ds(16, 16)], wsem.at[2]),
        pltpu.make_async_copy(down_hbm, down, wsem.at[3]),
        pltpu.make_async_copy(upq_hbm, upq.at[pl.ds(0, RANK)], wsem.at[4]),
        pltpu.make_async_copy(upv_hbm, upv.at[pl.ds(RANK, RANK)], wsem.at[5]),
        pltpu.make_async_copy(kc_hbm, kc, wsem.at[6]),
        pltpu.make_async_copy(vc_hbm, vc, wsem.at[7]),
        pltpu.make_async_copy(wo_hbm, wo, wsem.at[8]),
    ]
    for load in loads:
        load.start()

    barrier = pltpu.get_barrier_semaphore()
    for k in range(1, 8):
        other = (xc + k) % 8
        pl.semaphore_signal(barrier, inc=1, device_id={"wide": z * 8 + other}, device_id_type=MESH)
        pl.semaphore_signal(barrier, inc=1, device_id={"wide": ((z + k) % 8) * 8 + xc}, device_id_type=MESH)

    for k in (1, nseg - 1):
        pl.semaphore_signal(barrier, inc=1, device_id={"segment": (seg + k) % nseg}, device_id_type=MESH)
    pl.semaphore_wait(barrier, 16)

    pending = []

    def stage_one(number, send, mid, rows):
        dest = mid.at[:, pl.ds(pl.multiple_of(xc * rows, rows), rows), :]
        pltpu.make_async_copy(send.at[xc], dest, asem_r.at[number, 0]).start()
        for k in range(1, 8):
            other = (xc + k) % 8
            remote(send.at[other], dest, asem_s.at[number, 0], asem_r.at[number, 0], {"wide": z * 8 + other}).start()

    def stage_two(number, mid, recv, rows):
        pltpu.make_async_copy(mid, mid, asem_r.at[number, 0]).wait()
        mine = pl.ds(pl.multiple_of(z * 8 * rows, 8 * rows), 8 * rows)
        pltpu.make_async_copy(mid.at[z], recv.at[mine], asem_r.at[number, 1]).start()
        for k in range(1, 8):
            other = (z + k) % 8
            remote(
                mid.at[other], recv.at[mine], asem_s.at[number, 1], asem_r.at[number, 1], {"wide": other * 8 + xc}
            ).start()

    def arrived(number, send, mid, recv):
        pltpu.make_async_copy(recv, recv, asem_r.at[number, 1]).wait()
        pending.append(lambda: pltpu.make_async_copy(send.at[pl.ds(0, 7)], send.at[pl.ds(0, 7)], asem_s.at[number, 0]).wait())
        pending.append(lambda: pltpu.make_async_copy(mid.at[pl.ds(0, 7)], mid.at[pl.ds(0, 7)], asem_s.at[number, 1]).wait())

    def exchange(number, send, mid, swapped, recv):
        def rows(n):
            return pl.ds(pl.multiple_of(n * 32, 32), 32)

        pltpu.make_async_copy(send.at[rows(xc)], mid.at[rows(xc)], asem_r.at[number, 0]).start()
        for k in range(1, 8):
            other = (xc + k) % 8
            remote(
                send.at[rows(other)], mid.at[rows(xc)], asem_s.at[number, 0], asem_r.at[number, 0], {"wide": z * 8 + other}
            ).start()
        pltpu.make_async_copy(mid, mid, asem_r.at[number, 0]).wait()
        swapped[...] = dot(perm_b[...], mid[...]).astype(BF16)
        pltpu.make_async_copy(swapped.at[rows(z)], recv.at[rows(z)], asem_r.at[number, 1]).start()
        for k in range(1, 8):
            other = (z + k) % 8
            remote(
                swapped.at[rows(other)], recv.at[rows(z)], asem_s.at[number, 1], asem_r.at[number, 1], {"wide": other * 8 + xc}
            ).start()
        pltpu.make_async_copy(recv, recv, asem_r.at[number, 1]).wait()
        part = pl.ds(0, 224)
        pending.append(lambda: pltpu.make_async_copy(send.at[part], send.at[part], asem_s.at[number, 0]).wait())
        pending.append(lambda: pltpu.make_async_copy(swapped.at[part], swapped.at[part], asem_s.at[number, 1]).wait())

    def fold(dest, base):
        for m in range(16):
            dest[pl.ds(base, 16), m * 128:(m + 1) * 128] = tmp[pl.ds(m, 16, stride=16), :].astype(BF16)

    def unfold(source, base, dest, to):
        i, k = iota((64, 64), 0), iota((64, 64), 1)
        perm = onehot(k == ((i >> 2) & 3) * 16 + (i & 3) * 4 + (i >> 4))
        for part in range(4):
            moved = dot(perm, source[pl.ds(base, 64), part * 512:(part + 1) * 512]).astype(BF16)
            for q in range(4):
                dest[pl.ds(to, 16), q * 2048 + part * 512:q * 2048 + (part + 1) * 512] = moved[16 * q:16 * q + 16]

    ends = {0: [], 1: []}

    def gather(number, xb, fb, full):
        partner = wide(z, x, 1 - c)

        def block(xo, zo, half=None):
            at = pl.multiple_of((((x + xo) % XS) * ZS + (z + zo) % ZS) * 16, 16)
            return fb.at[pl.ds(at, 16), pl.ds(0, 2048) if half is None else pl.ds(half * 1024, 1024)]

        def chunk(zo, q):
            at = pl.multiple_of(((z + zo) % ZS) * 16, 16)
            return full.at[pl.ds(at, 16), pl.ds(q * 2048, 2048)]

        def share_a(zo, q):
            s = number, zo % ZS, q
            return remote(chunk(zo, q), chunk(zo, q), ua_s.at[s], ua_r.at[s], partner)

        def share_b(kind, zo):
            s = number, kind, zo % ZS
            at = block((0, 3, 1, 2, 2)[kind], zo, (None, None, None, 0, 1)[kind])
            return remote(at, at, ub_s.at[s], ub_r.at[s], partner)

        def spread(xo):
            for zh in range(2):
                xx = (x + xo) % XS
                unfold(
                    fb, pl.multiple_of((xx * ZS + zh * 4) * 16, 64), full, pl.multiple_of(128 + xx * 32 + zh * 16, 16)
                )

        @pl.when(c == 0)
        def _():
            sent = ends[0]

            def go(make, *args):
                make(*args).start()
                sent.append(lambda: make(*args).wait_send())

            def hop(k):
                own = xb.at[pl.ds(pl.multiple_of(x * 16, 16), 16)]
                return remote(own, own, xa_s.at[number, k - 1], xa_r.at[number, k - 1], wide(z, (x + k) % XS, c))

            fold(xb, pl.multiple_of(x * 16, 16))
            for k in range(1, XS):
                go(hop, k)
            for k in range(1, XS):
                hop(k).wait_recv()
            unfold(xb, 0, full, pl.multiple_of(z * 16, 16))

            def ring(direction, step, q):
                at = chunk(-step if direction == 0 else step, q)
                s = number, direction, step, q
                target = (z + (1 if direction == 0 else ZS - 1)) % ZS
                return remote(at, at, za_s.at[s], za_r.at[s], wide(target, x, c))

            def landed(direction, step, q):
                at = chunk(-(step + 1) if direction == 0 else step + 1, q)
                s = number, direction, step, q
                remote(at, at, za_s.at[s], za_r.at[s], partner).wait_recv()

            for q in range(4):
                for direction in range(2):
                    go(ring, direction, 0, q)
            for q in range(4):
                go(share_a, 0, q)
            for step in range(3):
                for q in range(4):
                    for direction in range(2):
                        landed(direction, step, q)
                        if step < 2 or q // 2 == direction:
                            go(ring, direction, step + 1, q)
                        go(share_a, -(step + 1) if direction == 0 else step + 1, q)
            for q in range(2):
                for direction in range(2):
                    landed(direction, 3, 2 * direction + q)
                    go(share_a, 4, 2 * direction + q)
            for kinds, xo in (((0,), 0), ((1,), 3), ((2,), 1), ((3, 4), 2)):
                for zo in range(ZS):
                    for kind in kinds:
                        share_b(kind, zo).wait_recv()
                spread(xo)

        @pl.when(c == 1)
        def _():
            sent = ends[1]

            def go(make, *args):
                make(*args).start()
                sent.append(lambda: make(*args).wait_send())

            def along_z(direction, step, half=None):
                at = block(0, -step if direction == 0 else step, half)
                s = number, direction, step
                target = (z + (1 if direction == 0 else ZS - 1)) % ZS
                return remote(at, at, zb_s.at[s], zb_r.at[s], wide(target, x, c))

            def from_z(direction, step, half=None):
                at = block(0, -(step + 1) if direction == 0 else step + 1, half)
                s = number, direction, step
                remote(at, at, zb_s.at[s], zb_r.at[s], partner).wait_recv()

            def along_x(direction, step, zo):
                at = block(0, zo) if step == 0 else block(3 if direction == 0 else 1, zo, direction)
                s = number, direction, step, zo % ZS
                target = (x + (1 if direction == 0 else XS - 1)) % XS
                return remote(at, at, xb_s.at[s], xb_r.at[s], wide(z, target, c))

            def from_x(direction, step, zo):
                at = block(3 if direction == 0 else 1, zo) if step == 0 else block(2, zo, direction)
                s = number, direction, step, zo % ZS
                remote(at, at, xb_s.at[s], xb_r.at[s], partner).wait_recv()

            def have(zo):
                go(along_x, 0, 0, zo)
                go(along_x, 1, 0, zo)
                go(share_b, 0, zo)

            def relay(zo):
                for direction in range(2):
                    from_x(direction, 0, zo)
                    go(along_x, direction, 1, zo)
                    go(share_b, 1 + direction, zo)

            fold(fb, pl.multiple_of((x * ZS + z) * 16, 16))
            go(along_z, 0, 0)
            go(along_z, 1, 0)
            have(0)
            for step in range(3):
                for direction in range(2):
                    from_z(direction, step)
                    go(along_z, direction, step + 1, None if step < 2 else direction)
                    have(-(step + 1) if direction == 0 else step + 1)
                if step == 0:
                    relay(0)
                else:
                    relay(-step)
                    relay(step)
            from_z(0, 3, 0)
            from_z(1, 3, 1)
            have(4)
            relay(-3)
            relay(3)
            spread(0)
            relay(4)
            spread(3)
            spread(1)
            for zo in (0, 7, 1, 6, 2, 5, 3, 4):
                for direction in range(2):
                    from_x(direction, 1, zo)
                    go(share_b, 3 + direction, zo)
            spread(2)
            for zo in range(ZS):
                for q in range(4):
                    share_a(zo, q).wait_recv()

    ix = jnp.broadcast_to(aux_ref[16:24, :][None], (8, 8, 128))
    for i in range(8):
        ix_send[i] = ix
    stage_one(0, ix_send, ix_mid, 8)
    stage_two(0, ix_mid, ix_recv, 8)

    wkv[32:128, :] = jnp.zeros((96, wkv.shape[1]), BF16)
    upq[RANK:2 * RANK, :] = jnp.zeros((RANK, upq.shape[1]), BF16)
    upv[0:RANK, :] = jnp.zeros((RANK, upv.shape[1]), BF16)

    arrived(0, ix_send, ix_mid, ix_recv)
    i, k = iota((256, 512), 0), iota((256, 512), 1)
    first = (((i >> 4) & 7) * XS + ((i >> 2) & 3)) * CS
    second = (((i >> 2) & 7) * XS + ((i >> 5) & 3)) * CS + 1
    source = jnp.where(i < 128, first, second) * 8 + (i & 3)
    column = dot(onehot(k == source), ix_recv[...].astype(BF16))
    row = column.T
    same = jnp.broadcast_to(column[:, 0:1], (256, 256)) == jnp.broadcast_to(row[0:1, :], (256, 256))
    before = same & (iota((256, 256), 1) < iota((256, 256), 0))
    order = jnp.sum(jnp.where(before, 1.0, 0.0), axis=1, keepdims=True)
    slot = (column[:, 0:1] * 16.0 + order).astype(jnp.int32)
    spots = iota((256, 1024), 1)
    tq[...] = onehot(spots == slot)
    tv[...] = onehot(spots == slot + 8)
    order_row = jnp.broadcast_to(order, (256, 128)).T
    i, k = iota((256, 256), 0), iota((256, 256), 1)
    zi, xi, ri = (i >> 2) & 7, i >> 6, i & 3
    perm_a[...] = onehot(k == jnp.where((i & 32) == 0, zi * 16 + xi * 4, 128 + xi * 32 + zi * 4) + ri)
    perm_b[...] = onehot(k == zi * 32 + (i >> 5) * 4 + ri)
    perm_c[...] = onehot(k == (i & 63) * 4 + (i >> 6))
    mine = (row[0:16, :].astype(jnp.int32) == me) & (order_row[0:16, :].astype(jnp.int32) == iota((16, 256), 0))
    chosen[...] = onehot(mine)

    @pl.when(seg == 0)
    def _():
        hst[...] = h0_ref[...].astype(F32)

    @pl.when(seg > 0)
    def _():
        remote(hout, hin, hsem.at[0], hsem.at[1], {"segment": seg - 1}).wait_recv()
        hst[...] = hin[...].astype(F32)

    gain = gain_ref[...]
    for r in range(4):
        block = hst[r * 64:(r + 1) * 64, :]
        total = jnp.sum(jnp.sum(block * block, axis=1, keepdims=True), axis=0, keepdims=True)
        tmp[r * 64:(r + 1) * 64, :] = block * lax.rsqrt(total * (1.0 / 8192.0) + EPS) * gain

    gather(0, xb1, fb1, xg)

    for n in range(6):
        loads[n].wait()
    acc_q[...] = jnp.zeros_like(acc_q)
    acc_kv[...] = jnp.zeros_like(acc_kv)
    acc_d[...] = jnp.zeros_like(acc_d)

    def column(n):
        return pl.ds(pl.multiple_of(n * 1024, 1024), 1024)

    @pl.loop(0, 8)
    def _(n):
        acc_d[...] += dot(xg[:, column(n)], down[column(n), :])

    low = dot(chosen[...], acc_d[...].astype(BF16)).astype(BF16)
    for part in range(8):
        q_slots = dot(low, upq[:, part * 1024:(part + 1) * 1024])
        v_slots = dot(low, upv[:, part * 128:(part + 1) * 128])
        for n in range(8):
            tile = jnp.concatenate([q_slots[0:8, n * 128:(n + 1) * 128], v_slots[0:8, :]], axis=0)
            co_send[n, part] = tile.astype(BF16)
    stage_one(1, co_send, co_mid, 16)

    @pl.loop(0, 8)
    def _(n):
        acc_q[...] += dot(xg[:, column(n)], wq[column(n), :])

    stage_two(1, co_mid, co_recv, 16)

    @pl.loop(0, 8)
    def _(n):
        acc_kv[...] += dot_nt(xg[:, column(n)], wkv[:, column(n)])

    arrived(1, co_send, co_mid, co_recv)

    a, b = iota((128, 128), 0), iota((128, 128), 1)
    moved = co_recv[...]
    query = acc_q[...] + 0.5 * dot(tq[...], moved)
    mine = onehot((b >= 16) & (b < 32) & (a == (xc * 16 - 16) + b))
    fresh = acc_kv[...] + 0.5 * dot(dot(tv[...], moved).astype(BF16), mine)
    qk_send[...] = dot(perm_a[...], jnp.concatenate([query.astype(BF16), fresh.astype(BF16)], axis=1)).astype(BF16)
    exchange(2, qk_send, qk_mid, qk_swap, qk_recv)
    rows_q[...] = dot(perm_c[...], qk_recv[...])

    loads[6].wait()
    loads[7].wait()
    spread_k = onehot(a == (b & 15))
    spread_v = onehot(a == (b & 15) + 16)
    a, b = iota((64, 128), 0), iota((64, 128), 1)
    lanes = (b >> 4) == (a & 7)
    a, b = iota((64, 64), 0), iota((64, 64), 1)
    heads = onehot((a >> 3) == (b >> 3))
    a, b = iota((64, 1024), 0), iota((64, 1024), 1)
    diagonal = (b >> 7) == (a >> 3)
    past = iota((64, 384), 1)
    scale = HD ** (-0.5)
    for r in range(4):
        cosine, sine = aux_ref[r:r + 1, :], aux_ref[4 + r:5 + r, :]
        length = aux_ref[8 + r:9 + r, 0:1].astype(jnp.int32)
        q_row = rows_q[r * 64:(r + 1) * 64, 0:128]
        kv_row = rows_q[r * 64:(r + 1) * 64, 128:256].astype(BF16)
        k_row = dot(heads, jnp.where(lanes, dot(kv_row, spread_k), 0.0).astype(BF16))
        v_row = dot(heads, jnp.where(lanes, dot(kv_row, spread_v), 0.0).astype(BF16))
        q_rot = (q_row * cosine + pltpu.roll(q_row, 64, 1) * sine).astype(BF16).astype(F32)
        k_rot = (k_row * cosine + pltpu.roll(k_row, 64, 1) * sine).astype(BF16).astype(F32)
        own = jnp.sum(q_rot * k_rot, axis=1, keepdims=True) * scale
        wide_q = jnp.where(diagonal, jnp.concatenate([q_rot] * 8, axis=1), 0.0).astype(BF16)
        scores = dot_nt(wide_q, kc[r * 384:(r + 1) * 384, :]) * scale
        valid = past < length
        scores = jnp.where(valid, scores, -1e30)
        top = jnp.maximum(jnp.max(scores, axis=1, keepdims=True), own)
        powers = jnp.where(valid, jnp.exp(scores - top), 0.0)
        own_power = jnp.exp(own - top)
        total = jnp.sum(powers, axis=1, keepdims=True) + own_power
        weights = (powers / total).astype(BF16)
        own_weight = (own_power / total).astype(BF16).astype(F32)
        mixed = dot(weights, vc[r * 384:(r + 1) * 384, :])
        mixed = jnp.concatenate([mixed[8 * g:8 * g + 8, 128 * g:128 * g + 128] for g in range(8)], axis=0)
        tmp[r * 64:(r + 1) * 64, :] = mixed + own_weight * v_row

    gather(1, xb2, fb2, ag)

    loads[8].wait()
    acc_q[...] = jnp.zeros_like(acc_q)

    @pl.loop(0, 8)
    def _(n):
        part = pl.ds(pl.multiple_of(n * 1024, 1024), 1024)
        acc_q[...] += dot(ag[:, part], wo[part, :])

    ou_send[...] = dot(perm_a[...], acc_q[...].astype(BF16)).astype(BF16)
    exchange(3, ou_send, ou_mid, ou_swap, ou_recv)
    projected = dot(perm_c[...], ou_recv[...])
    for r in range(4):
        rows = slice(r * 64, (r + 1) * 64)
        result = (hst[rows, :] + projected[rows, :]).astype(BF16)
        out_ref[rows, :] = result
        hout[rows, :] = result

    @pl.when(seg < nseg - 1)
    def _():
        passing = remote(hout, hin, hsem.at[0], hsem.at[1], {"segment": seg + 1})
        passing.start()
        passing.wait_send()

    for wait in pending:
        wait()
    for core in range(CS):
        @pl.when(c == core)
        def _(core=core):
            for wait in ends[core]:
                wait()


def on_device(
    entering_hidden, row_adapter_index, lengths, input_norm_gain, query_matrix, key_matrix, value_matrix,
    output_matrix, adapter_down_maps, adapter_up_query, adapter_up_value, rotated_key_cache, cached_values,
):
    half = HD // 2
    positions = lengths.reshape(4, 1).astype(F32)
    inverse = ROPE_BASE ** (-jnp.arange(half, dtype=F32) / half)
    angles = positions * inverse[None, :]
    cosine, sine = jnp.cos(angles), jnp.sin(angles)
    spread = lambda v: jnp.pad(jnp.broadcast_to(v, (4, 128)), ((0, 4), (0, 0)))
    aux = jnp.concatenate(
        [
            jnp.concatenate([cosine, cosine], 1),
            jnp.concatenate([-sine, sine], 1),
            spread(positions),
            spread(row_adapter_index.reshape(4, 1).astype(F32)),
        ],
        0,
    )
    vmem = pl.BlockSpec(memory_space=pltpu.VMEM)
    hbm = pl.BlockSpec(memory_space=pl.ANY)
    tiles = lambda rows, kind: [
        pltpu.VMEM((8, 8, rows, 128), kind), pltpu.VMEM((8, 8 * rows, 128), kind), pltpu.VMEM((64 * rows, 128), kind)
    ]
    dma = pltpu.SemaphoreType.DMA
    out = pl.pallas_call(
        kernel,
        out_shape=jax.ShapeDtypeStruct((256, 128), BF16),
        in_specs=[vmem] * 3 + [hbm] * 9,
        out_specs=vmem,
        scratch_shapes=[
            pltpu.VMEM((8192, 128), BF16), pltpu.VMEM((128, 8192), BF16), pltpu.VMEM((8192, 128), BF16),
            pltpu.VMEM((8192, 128), BF16), pltpu.VMEM((128, 8192), BF16), pltpu.VMEM((128, 1024), BF16),
            pltpu.VMEM((1536, 1024), BF16), pltpu.VMEM((1536, 1024), BF16),
            pltpu.VMEM((256, 128), F32), pltpu.VMEM((256, 128), F32),
            pltpu.VMEM((256, 128), BF16), pltpu.VMEM((256, 128), BF16),
            pltpu.VMEM((64, 2048), BF16), pltpu.VMEM((64, 2048), BF16),
            pltpu.VMEM((512, 2048), BF16), pltpu.VMEM((512, 2048), BF16),
            pltpu.VMEM((256, 8192), BF16), pltpu.VMEM((256, 8192), BF16),
            pltpu.VMEM((256, 128), F32), pltpu.VMEM((256, 128), F32), pltpu.VMEM((256, 128), F32),
            *tiles(8, F32), *tiles(16, BF16),
            *[pltpu.VMEM((256, 256), BF16)] * 4, *[pltpu.VMEM((256, 128), BF16)] * 4,
            pltpu.VMEM((256, 1024), BF16), pltpu.VMEM((256, 1024), BF16), pltpu.VMEM((16, 256), BF16),
            *[pltpu.VMEM((256, 256), BF16)] * 3, pltpu.VMEM((256, 256), F32),
            dma((9,)), *[dma((2, 3))] * 2, *[dma((2, 2, 4, 4))] * 2, *[dma((2, 8, 4))] * 2,
            *[dma((2, 2, 4))] * 2, *[dma((2, 2, 2, 8))] * 2, *[dma((2, 5, 8))] * 2, dma((4, 2)), dma((4, 2)), dma((2,)),
        ],
        compiler_params=pltpu.CompilerParams(
            collective_id=0, has_side_effects=True, vmem_limit_bytes=60 * 1024 * 1024
        ),
        name="layer_step",
    )(
        entering_hidden.reshape(256, 128),
        aux,
        input_norm_gain.astype(F32).reshape(64, 128),
        query_matrix[0],
        key_matrix[0].T,
        value_matrix[0].T,
        output_matrix[0],
        adapter_down_maps[0, 0],
        adapter_up_query[0, 0],
        adapter_up_value[0, 0],
        rotated_key_cache.reshape(1536, 1024),
        cached_values.reshape(1536, 1024),
    )
    return out.reshape(1, 2, 2, 8192)


def solution(mesh):
    placed = (
        P(None, "wide", None), P(None, "wide", None), P(None, "wide"), P("segment", None),
        P("segment", None, "wide"), P("segment", None, "wide"), P("segment", None, "wide"), P("segment", None, "wide"),
        P("segment", "wide", None, None), P("segment", "wide", None, None), P("segment", "wide", None, None),
        P("segment", None, "wide", None, None), P("segment", None, "wide", None, None),
    )
    return jax.shard_map(
        on_device, mesh=mesh, in_specs=placed, out_specs=P("segment", None, "wide", None), check_vma=False
    )
```

```python
import jax
import jax.numpy as jnp
from jax import lax
from jax.experimental import pallas as pl
from jax.experimental.pallas import tpu as pltpu
from jax.sharding import PartitionSpec as P

HD = 128
RANK = 64
EPS = 1e-05
ROPE_BASE = 500000.0
ZS, XS, CS = 8, 4, 2
MESH = pl.DeviceIdType.MESH
F32 = jnp.float32
BF16 = jnp.bfloat16


def iota(shape, dim):
    return lax.broadcasted_iota(jnp.int32, shape, dim)


def onehot(cond):
    return jnp.where(cond, 1.0, 0.0).astype(BF16)


def dot(a, b):
    return jnp.dot(a, b, preferred_element_type=F32)


def dot_nt(a, b):
    return lax.dot_general(a, b, (((1,), (1,)), ((), ())), preferred_element_type=F32)


def kernel(
    h0_ref, aux_ref, gain_ref, wq_hbm, wk_hbm, wv_hbm, wo_hbm, down_hbm, upq_hbm, upv_hbm, kc_hbm, vc_hbm,
    out_ref,
    wq, wkv, wo, down, upq, upv, kc, vc,
    hst, tmp, hin, hres,
    xb1, xb2, fb1, fb2, xg, ag, acc_q, acc_kv, acc_d,
    ix_send, ix_mid, ix_recv, co_send, co_mid, co_swap, co_recv, qk_send, qk_mid, qk_swap, qk_recv, ou_send, ou_mid, ou_swap, ou_recv, ou_next,
    tq, tv, chosen, vmask, perm_a, perm_b, perm_c, perm_s, rows_q,
    wsem, xa_s, xa_r, za_s, za_r, ua_s, ua_r, zb_s, zb_r, xb_s, xb_r, ub_s, ub_r, asem_s, asem_r, hsem, nsem,
):
    seg = lax.axis_index("segment")
    me = lax.axis_index("wide")
    nseg = lax.axis_size("segment")
    z = me // (XS * CS)
    xc = me % (XS * CS)
    x = xc // CS
    c = xc % CS
    grp = z * CS + c

    def wide(zz, xx, cc):
        return {"wide": (zz * XS + xx) * CS + cc}

    def remote(src, dst, ssem, rsem, dev):
        return pltpu.make_async_remote_copy(
            src_ref=src, dst_ref=dst, send_sem=ssem, recv_sem=rsem, device_id=dev, device_id_type=MESH
        )

    loads = [
        pltpu.make_async_copy(wq_hbm, wq, wsem.at[0]),
        pltpu.make_async_copy(wk_hbm, wkv.at[pl.ds(0, 16)], wsem.at[1]),
        pltpu.make_async_copy(wv_hbm, wkv.at[pl.ds(16, 16)], wsem.at[2]),
        pltpu.make_async_copy(down_hbm, down, wsem.at[3]),
        pltpu.make_async_copy(upq_hbm, upq.at[pl.ds(0, RANK)], wsem.at[4]),
        pltpu.make_async_copy(upv_hbm, upv.at[pl.ds(RANK, RANK)], wsem.at[5]),
        pltpu.make_async_copy(kc_hbm, kc, wsem.at[6]),
        pltpu.make_async_copy(vc_hbm, vc, wsem.at[7]),
        pltpu.make_async_copy(wo_hbm, wo, wsem.at[8]),
    ]
    for load in loads:
        load.start()

    barrier = pltpu.get_barrier_semaphore()
    for k in range(1, 8):
        other = (xc + k) % 8
        pl.semaphore_signal(barrier, inc=1, device_id={"wide": z * 8 + other}, device_id_type=MESH)
        pl.semaphore_signal(barrier, inc=1, device_id={"wide": ((z + k) % 8) * 8 + xc}, device_id_type=MESH)

    for k in (1, nseg - 1):
        for other in range(8):
            pl.semaphore_signal(
                barrier, inc=1, device_id={"segment": (seg + k) % nseg, "wide": other * 8 + xc}, device_id_type=MESH
            )
    pl.semaphore_wait(barrier, 30)

    pending = []

    def stage_one(number, send, mid, rows):
        dest = mid.at[:, pl.ds(pl.multiple_of(xc * rows, rows), rows), :]
        pltpu.make_async_copy(send.at[xc], dest, asem_r.at[number, 0]).start()
        for k in range(1, 8):
            other = (xc + k) % 8
            remote(send.at[other], dest, asem_s.at[number, 0], asem_r.at[number, 0], {"wide": z * 8 + other}).start()

    def stage_two(number, mid, recv, rows):
        pltpu.make_async_copy(mid, mid, asem_r.at[number, 0]).wait()
        mine = pl.ds(pl.multiple_of(z * 8 * rows, 8 * rows), 8 * rows)
        pltpu.make_async_copy(mid.at[z], recv.at[mine], asem_r.at[number, 1]).start()
        for k in range(1, 8):
            other = (z + k) % 8
            remote(
                mid.at[other], recv.at[mine], asem_s.at[number, 1], asem_r.at[number, 1], {"wide": other * 8 + xc}
            ).start()

    for side, ref in enumerate((ix_send, ix_mid)):
        pending.append(
            lambda side=side, ref=ref: pltpu.make_async_copy(ref.at[pl.ds(0, 7)], ref.at[pl.ds(0, 7)], asem_s.at[0, side]).wait()
        )

    def in_plane(number, send, mid, count):
        def rows(n):
            return pl.ds(pl.multiple_of(n * count, 16), count)

        pltpu.make_async_copy(send.at[rows(xc)], mid.at[rows(xc)], asem_r.at[number, 0]).start()
        for k in range(1, 8):
            other = (xc + k) % 8
            remote(
                send.at[rows(other)], mid.at[rows(xc)], asem_s.at[number, 0], asem_r.at[number, 0], {"wide": z * 8 + other}
            ).start()

    def in_plane_done(number, mid):
        pltpu.make_async_copy(mid, mid, asem_r.at[number, 0]).wait()

    def along_line(number, swapped, recv, count):
        def rows(n):
            return pl.ds(pl.multiple_of(n * count, 16), count)

        pltpu.make_async_copy(swapped.at[rows(z)], recv.at[rows(z)], asem_r.at[number, 1]).start()
        for k in range(1, 8):
            other = (z + k) % 8
            remote(
                swapped.at[rows(other)], recv.at[rows(z)], asem_s.at[number, 1], asem_r.at[number, 1], {"wide": other * 8 + xc}
            ).start()

    def along_line_done(number, send, swapped, recv, count):
        pltpu.make_async_copy(recv, recv, asem_r.at[number, 1]).wait()
        part = pl.ds(0, 7 * count)
        pending.append(lambda: pltpu.make_async_copy(send.at[part], send.at[part], asem_s.at[number, 0]).wait())
        pending.append(lambda: pltpu.make_async_copy(swapped.at[part], swapped.at[part], asem_s.at[number, 1]).wait())

    def block_swap(tiles):
        block = iota((8, 128), 1) >> 4
        shifted = [[pltpu.roll(t, 16 * k, 1) if k else t for t in tiles] for k in range(8)]
        swapped = []
        for p in range(8):
            total = jnp.zeros((8, 128), F32)
            for k in range(8):
                total = jnp.where(block == (p + k) % 8, shifted[k][(p + k) % 8], total)
            swapped.append(jnp.concatenate([total, jnp.zeros((8, 128), F32)], axis=0).astype(BF16))
        return swapped

    def fold(dest, base):
        for m in range(16):
            dest[pl.ds(base, 16), m * 128:(m + 1) * 128] = tmp[pl.ds(m, 16, stride=16), :].astype(BF16)

    def unfold(source, base, dest, to):
        i, k = iota((64, 64), 0), iota((64, 64), 1)
        perm = onehot(k == ((i >> 2) & 3) * 16 + (i & 3) * 4 + (i >> 4))
        for part in range(4):
            moved = dot(perm, source[pl.ds(base, 64), part * 512:(part + 1) * 512]).astype(BF16)
            for q in range(4):
                dest[pl.ds(to, 16), q * 2048 + part * 512:q * 2048 + (part + 1) * 512] = moved[16 * q:16 * q + 16]

    ends = {0: [], 1: []}

    def gather(number, xb, fb, full):
        partner = wide(z, x, 1 - c)

        def block(xo, zo, half=None):
            at = pl.multiple_of((((x + xo) % XS) * ZS + (z + zo) % ZS) * 16, 16)
            return fb.at[pl.ds(at, 16), pl.ds(0, 2048) if half is None else pl.ds(half * 1024, 1024)]

        def chunk(zo, q):
            at = pl.multiple_of(((z + zo) % ZS) * 16, 16)
            return full.at[pl.ds(at, 16), pl.ds(q * 2048, 2048)]

        def share_a(zo, q):
            s = number, zo % ZS, q
            return remote(chunk(zo, q), chunk(zo, q), ua_s.at[s], ua_r.at[s], partner)

        def share_b(kind, zo):
            s = number, kind, zo % ZS
            at = block((0, 3, 1, 2, 2)[kind], zo, (None, None, None, 0, 1)[kind])
            return remote(at, at, ub_s.at[s], ub_r.at[s], partner)

        def spread(xo):
            for zh in range(2):
                xx = (x + xo) % XS
                unfold(
                    fb, pl.multiple_of((xx * ZS + zh * 4) * 16, 64), full, pl.multiple_of(128 + xx * 32 + zh * 16, 16)
                )

        @pl.when(c == 0)
        def _():
            sent = ends[0]

            def go(make, *args):
                make(*args).start()
                sent.append(lambda: make(*args).wait_send())

            def hop(k):
                own = xb.at[pl.ds(pl.multiple_of(x * 16, 16), 16)]
                return remote(own, own, xa_s.at[number, k - 1], xa_r.at[number, k - 1], wide(z, (x + k) % XS, c))

            fold(xb, pl.multiple_of(x * 16, 16))
            for k in range(1, XS):
                go(hop, k)
            for k in range(1, XS):
                hop(k).wait_recv()
            unfold(xb, 0, full, pl.multiple_of(z * 16, 16))

            def ring(direction, step, q):
                at = chunk(-step if direction == 0 else step, q)
                s = number, direction, step, q
                target = (z + (1 if direction == 0 else ZS - 1)) % ZS
                return remote(at, at, za_s.at[s], za_r.at[s], wide(target, x, c))

            def landed(direction, step, q):
                at = chunk(-(step + 1) if direction == 0 else step + 1, q)
                s = number, direction, step, q
                remote(at, at, za_s.at[s], za_r.at[s], partner).wait_recv()

            for q in range(4):
                for direction in range(2):
                    go(ring, direction, 0, q)
            for q in range(4):
                go(share_a, 0, q)
            for step in range(3):
                for q in range(4):
                    for direction in range(2):
                        landed(direction, step, q)
                        if step < 2 or q // 2 == direction:
                            go(ring, direction, step + 1, q)
                        go(share_a, -(step + 1) if direction == 0 else step + 1, q)
            for q in range(2):
                for direction in range(2):
                    landed(direction, 3, 2 * direction + q)
                    go(share_a, 4, 2 * direction + q)
            for kinds, xo in (((0,), 0), ((1,), 3), ((2,), 1), ((3, 4), 2)):
                for zo in range(ZS):
                    for kind in kinds:
                        share_b(kind, zo).wait_recv()
                spread(xo)

        @pl.when(c == 1)
        def _():
            sent = ends[1]

            def go(make, *args):
                make(*args).start()
                sent.append(lambda: make(*args).wait_send())

            def along_z(direction, step, half=None):
                at = block(0, -step if direction == 0 else step, half)
                s = number, direction, step
                target = (z + (1 if direction == 0 else ZS - 1)) % ZS
                return remote(at, at, zb_s.at[s], zb_r.at[s], wide(target, x, c))

            def from_z(direction, step, half=None):
                at = block(0, -(step + 1) if direction == 0 else step + 1, half)
                s = number, direction, step
                remote(at, at, zb_s.at[s], zb_r.at[s], partner).wait_recv()

            def along_x(direction, step, zo):
                at = block(0, zo) if step == 0 else block(3 if direction == 0 else 1, zo, direction)
                s = number, direction, step, zo % ZS
                target = (x + (1 if direction == 0 else XS - 1)) % XS
                return remote(at, at, xb_s.at[s], xb_r.at[s], wide(z, target, c))

            def from_x(direction, step, zo):
                at = block(3 if direction == 0 else 1, zo) if step == 0 else block(2, zo, direction)
                s = number, direction, step, zo % ZS
                remote(at, at, xb_s.at[s], xb_r.at[s], partner).wait_recv()

            def have(zo):
                go(along_x, 0, 0, zo)
                go(along_x, 1, 0, zo)
                go(share_b, 0, zo)

            def relay(zo):
                for direction in range(2):
                    from_x(direction, 0, zo)
                    go(along_x, direction, 1, zo)
                    go(share_b, 1 + direction, zo)

            fold(fb, pl.multiple_of((x * ZS + z) * 16, 16))
            go(along_z, 0, 0)
            go(along_z, 1, 0)
            have(0)
            for step in range(3):
                for direction in range(2):
                    from_z(direction, step)
                    go(along_z, direction, step + 1, None if step < 2 else direction)
                    have(-(step + 1) if direction == 0 else step + 1)
                if step == 0:
                    relay(0)
                else:
                    relay(-step)
                    relay(step)
            from_z(0, 3, 0)
            from_z(1, 3, 1)
            have(4)
            relay(-3)
            relay(3)
            spread(0)
            relay(4)
            spread(3)
            spread(1)
            for zo in (0, 7, 1, 6, 2, 5, 3, 4):
                for direction in range(2):
                    from_x(direction, 1, zo)
                    go(share_b, 3 + direction, zo)
            spread(2)
            for zo in range(ZS):
                for q in range(4):
                    share_a(zo, q).wait_recv()

    ix = jnp.broadcast_to(aux_ref[16:24, :][None], (8, 8, 128))
    for i in range(8):
        ix_send[i] = ix
    stage_one(0, ix_send, ix_mid, 8)

    def prepare():
        wkv[32:128, :] = jnp.zeros((96, wkv.shape[1]), BF16)
        upq[RANK:2 * RANK, :] = jnp.zeros((RANK, upq.shape[1]), BF16)
        upv[0:RANK, :] = jnp.zeros((RANK, upv.shape[1]), BF16)
        i, k = iota((256, 256), 0), iota((256, 256), 1)
        zi, xi, ri = (i >> 2) & 7, i >> 6, i & 3
        perm_a[...] = onehot(k == jnp.where((i & 32) == 0, zi * 16 + xi * 4, 128 + xi * 32 + zi * 4) + ri)
        perm_b[...] = onehot(k == zi * 32 + (i >> 5) * 4 + ri)
        perm_c[...] = onehot(k == (i & 63) * 4 + (i >> 6))
        i, k = iota((512, 640), 0), iota((512, 640), 1)
        perm_s[...] = onehot(k == ((i >> 3) & 7) * 80 + (i >> 6) * 8 + (i & 7))
        pltpu.make_async_copy(ix_recv, ix_recv, asem_r.at[0, 1]).wait()
        i, k = iota((256, 512), 0), iota((256, 512), 1)
        first = (((i >> 4) & 7) * XS + ((i >> 2) & 3)) * CS
        second = (((i >> 2) & 7) * XS + ((i >> 5) & 3)) * CS + 1
        source = jnp.where(i < 128, first, second) * 8 + (i & 3)
        names = dot(onehot(k == source), ix_recv[...].astype(BF16))
        row = names.T
        same = jnp.broadcast_to(names[:, 0:1], (256, 256)) == jnp.broadcast_to(row[0:1, :], (256, 256))
        before = same & (iota((256, 256), 1) < iota((256, 256), 0))
        order = jnp.sum(jnp.where(before, 1.0, 0.0), axis=1, keepdims=True)
        name = names[:, 0:1].astype(jnp.int32)
        at = (name >> 3) * 80 + order.astype(jnp.int32)
        spots = iota((256, 640), 1)
        tq[...] = onehot(spots == at + (name & 7) * 8)
        tv[...] = onehot(spots == at + 64)
        vmask[...] = jnp.where((iota((256, 128), 1) >> 4) == (names.astype(jnp.int32) & 7), 1.0, 0.0)
        order_row = jnp.broadcast_to(order, (256, 128)).T
        mine = (row[0:16, :].astype(jnp.int32) == me) & (order_row[0:16, :].astype(jnp.int32) == iota((16, 256), 0))
        chosen[...] = onehot(mine)

    def passing():
        return remote(hres, hin, hsem.at[0], hsem.at[1], {"segment": (seg + 1) % nseg})

    @pl.when(seg == 0)
    def _():
        hres[...] = h0_ref[...]
        hst[...] = h0_ref[...].astype(F32)

    @pl.when(seg > 0)
    def _():
        stage_two(0, ix_mid, ix_recv, 8)
        prepare()
        passing().wait_recv()
        pltpu.make_async_copy(ou_next, ou_next, nsem.at[1]).wait()
        for r in range(4):
            rows = slice(r * 64, (r + 1) * 64)
            result = (hin[rows, :].astype(F32) + dot(perm_c[rows, :], ou_next[...])).astype(BF16)
            hres[rows, :] = result
            hst[rows, :] = result.astype(F32)

    gain = gain_ref[...]
    for r in range(4):
        block = hst[r * 64:(r + 1) * 64, :]
        total = jnp.sum(jnp.sum(block * block, axis=1, keepdims=True), axis=0, keepdims=True)
        tmp[r * 64:(r + 1) * 64, :] = block * lax.rsqrt(total * (1.0 / 8192.0) + EPS) * gain

    @pl.when(seg < nseg - 1)
    def _():
        passing().start()

    gather(0, xb1, fb1, xg)

    @pl.when(seg == 0)
    def _():
        stage_two(0, ix_mid, ix_recv, 8)


    for n in range(6):
        loads[n].wait()
    acc_q[...] = jnp.zeros_like(acc_q)
    acc_kv[...] = jnp.zeros_like(acc_kv)
    acc_d[...] = jnp.zeros_like(acc_d)

    def column(n):
        return pl.ds(pl.multiple_of(n * 1024, 1024), 1024)

    @pl.loop(0, 8)
    def _(n):
        acc_d[...] += dot(xg[:, column(n)], down[column(n), :])

    @pl.when(seg == 0)
    def _():
        prepare()

    low = dot(chosen[...], acc_d[...].astype(BF16)).astype(BF16)
    values = []
    for part in range(0, 8, 2):
        q_slots = [dot(low, upq[:, (part + n) * 1024:(part + n + 1) * 1024])[0:8] for n in range(2)]
        values += [dot(low, upv[:, (part + n) * 128:(part + n + 1) * 128])[0:8] for n in range(2)]
        for n in range(8):
            tile = jnp.concatenate([q[:, n * 128:(n + 1) * 128] for q in q_slots], axis=0)
            co_send[n * 80 + part * 8:n * 80 + part * 8 + 16, :] = tile.astype(BF16)
    for n, tile in enumerate(block_swap(values)):
        co_send[n * 80 + 64:n * 80 + 80, :] = tile
    in_plane(1, co_send, co_mid, 80)

    @pl.loop(0, 8)
    def _(n):
        acc_q[...] += dot(xg[:, column(n)], wq[column(n), :])

    in_plane_done(1, co_mid)
    swapped = dot(perm_s[...], co_mid[...]).astype(BF16)
    values = [co_mid[n * 80 + 64:n * 80 + 80, :].astype(F32)[0:8] for n in range(8)]
    for n, tile in enumerate(block_swap(values)):
        co_swap[n * 80:n * 80 + 64, :] = swapped[n * 64:(n + 1) * 64]
        co_swap[n * 80 + 64:n * 80 + 80, :] = tile
    along_line(1, co_swap, co_recv, 80)

    @pl.loop(0, 8)
    def _(n):
        acc_kv[...] += dot_nt(xg[:, column(n)], wkv[:, column(n)])

    along_line_done(1, co_send, co_swap, co_recv, 80)

    a, b = iota((128, 128), 0), iota((128, 128), 1)
    moved = co_recv[...]
    query = acc_q[...] + 0.5 * dot(tq[...], moved)
    narrow = onehot((b >= 16) & (b < 32) & ((a & 15) == b - 16))
    fresh = acc_kv[...] + 0.5 * dot((dot(tv[...], moved) * vmask[...]).astype(BF16), narrow)
    qk_send[...] = dot(perm_a[...], jnp.concatenate([query.astype(BF16), fresh.astype(BF16)], axis=1)).astype(BF16)
    in_plane(2, qk_send, qk_mid, 32)
    in_plane_done(2, qk_mid)
    qk_swap[...] = dot(perm_b[...], qk_mid[...]).astype(BF16)
    along_line(2, qk_swap, qk_recv, 32)
    along_line_done(2, qk_send, qk_swap, qk_recv, 32)
    rows_q[...] = dot(perm_c[...], qk_recv[...])

    loads[6].wait()
    loads[7].wait()
    spread_k = onehot(a == (b & 15))
    spread_v = onehot(a == (b & 15) + 16)
    a, b = iota((64, 128), 0), iota((64, 128), 1)
    lanes = (b >> 4) == (a & 7)
    a, b = iota((64, 64), 0), iota((64, 64), 1)
    heads = onehot((a >> 3) == (b >> 3))
    a, b = iota((64, 1024), 0), iota((64, 1024), 1)
    diagonal = (b >> 7) == (a >> 3)
    past = iota((64, 384), 1)
    scale = HD ** (-0.5)
    for r in range(4):
        cosine, sine = aux_ref[r:r + 1, :], aux_ref[4 + r:5 + r, :]
        length = aux_ref[8 + r:9 + r, 0:1].astype(jnp.int32)
        q_row = rows_q[r * 64:(r + 1) * 64, 0:128]
        kv_row = rows_q[r * 64:(r + 1) * 64, 128:256].astype(BF16)
        k_row = dot(heads, jnp.where(lanes, dot(kv_row, spread_k), 0.0).astype(BF16))
        v_row = dot(heads, jnp.where(lanes, dot(kv_row, spread_v), 0.0).astype(BF16))
        q_rot = (q_row * cosine + pltpu.roll(q_row, 64, 1) * sine).astype(BF16).astype(F32)
        k_rot = (k_row * cosine + pltpu.roll(k_row, 64, 1) * sine).astype(BF16).astype(F32)
        own = jnp.sum(q_rot * k_rot, axis=1, keepdims=True) * scale
        wide_q = jnp.where(diagonal, jnp.concatenate([q_rot] * 8, axis=1), 0.0).astype(BF16)
        scores = dot_nt(wide_q, kc[r * 384:(r + 1) * 384, :]) * scale
        valid = past < length
        scores = jnp.where(valid, scores, -1e30)
        top = jnp.maximum(jnp.max(scores, axis=1, keepdims=True), own)
        powers = jnp.where(valid, jnp.exp(scores - top), 0.0)
        own_power = jnp.exp(own - top)
        total = jnp.sum(powers, axis=1, keepdims=True) + own_power
        weights = (powers / total).astype(BF16)
        own_weight = (own_power / total).astype(BF16).astype(F32)
        mixed = dot(weights, vc[r * 384:(r + 1) * 384, :])
        mixed = jnp.concatenate([mixed[8 * g:8 * g + 8, 128 * g:128 * g + 128] for g in range(8)], axis=0)
        tmp[r * 64:(r + 1) * 64, :] = mixed + own_weight * v_row

    gather(1, xb2, fb2, ag)

    loads[8].wait()
    acc_q[...] = jnp.zeros_like(acc_q)

    @pl.loop(0, 8)
    def _(n):
        part = pl.ds(pl.multiple_of(n * 1024, 1024), 1024)
        acc_q[...] += dot(ag[:, part], wo[part, :])

    ou_send[...] = dot(perm_a[...], acc_q[...].astype(BF16)).astype(BF16)
    in_plane(3, ou_send, ou_mid, 32)
    in_plane_done(3, ou_mid)
    ou_swap[...] = dot(perm_b[...], ou_mid[...]).astype(BF16)

    @pl.when(seg < nseg - 1)
    def _():
        for k in range(8):
            other = (z + k) % 8
            remote(
                ou_swap.at[pl.ds(pl.multiple_of(other * 32, 32), 32)], ou_next.at[pl.ds(pl.multiple_of(z * 32, 32), 32)],
                nsem.at[0], nsem.at[1], {"segment": seg + 1, "wide": other * 8 + xc},
            ).start()

    along_line(3, ou_swap, ou_recv, 32)
    along_line_done(3, ou_send, ou_swap, ou_recv, 32)
    for r in range(4):
        rows = slice(r * 64, (r + 1) * 64)
        out_ref[rows, :] = (hst[rows, :] + dot(perm_c[rows, :], ou_recv[...])).astype(BF16)

    @pl.when(seg < nseg - 1)
    def _():
        passing().wait_send()
        pltpu.make_async_copy(ou_swap, ou_swap, nsem.at[0]).wait()

    for wait in pending:
        wait()
    for core in range(CS):
        @pl.when(c == core)
        def _(core=core):
            for wait in ends[core]:
                wait()


def on_device(
    entering_hidden, row_adapter_index, lengths, input_norm_gain, query_matrix, key_matrix, value_matrix,
    output_matrix, adapter_down_maps, adapter_up_query, adapter_up_value, rotated_key_cache, cached_values,
):
    half = HD // 2
    positions = lengths.reshape(4, 1).astype(F32)
    inverse = ROPE_BASE ** (-jnp.arange(half, dtype=F32) / half)
    angles = positions * inverse[None, :]
    cosine, sine = jnp.cos(angles), jnp.sin(angles)
    spread = lambda v: jnp.pad(jnp.broadcast_to(v, (4, 128)), ((0, 4), (0, 0)))
    aux = jnp.concatenate(
        [
            jnp.concatenate([cosine, cosine], 1),
            jnp.concatenate([-sine, sine], 1),
            spread(positions),
            spread(row_adapter_index.reshape(4, 1).astype(F32)),
        ],
        0,
    )
    vmem = pl.BlockSpec(memory_space=pltpu.VMEM)
    hbm = pl.BlockSpec(memory_space=pl.ANY)
    tiles = lambda rows, kind: [
        pltpu.VMEM((8, 8, rows, 128), kind), pltpu.VMEM((8, 8 * rows, 128), kind), pltpu.VMEM((64 * rows, 128), kind)
    ]
    dma = pltpu.SemaphoreType.DMA
    out = pl.pallas_call(
        kernel,
        out_shape=jax.ShapeDtypeStruct((256, 128), BF16),
        in_specs=[vmem] * 3 + [hbm] * 9,
        out_specs=vmem,
        scratch_shapes=[
            pltpu.VMEM((8192, 128), BF16), pltpu.VMEM((128, 8192), BF16), pltpu.VMEM((8192, 128), BF16),
            pltpu.VMEM((8192, 128), BF16), pltpu.VMEM((128, 8192), BF16), pltpu.VMEM((128, 1024), BF16),
            pltpu.VMEM((1536, 1024), BF16), pltpu.VMEM((1536, 1024), BF16),
            pltpu.VMEM((256, 128), F32), pltpu.VMEM((256, 128), F32),
            pltpu.VMEM((256, 128), BF16), pltpu.VMEM((256, 128), BF16),
            pltpu.VMEM((64, 2048), BF16), pltpu.VMEM((64, 2048), BF16),
            pltpu.VMEM((512, 2048), BF16), pltpu.VMEM((512, 2048), BF16),
            pltpu.VMEM((256, 8192), BF16), pltpu.VMEM((256, 8192), BF16),
            pltpu.VMEM((256, 128), F32), pltpu.VMEM((256, 128), F32), pltpu.VMEM((256, 128), F32),
            *tiles(8, F32), *[pltpu.VMEM((640, 128), BF16)] * 4,
            *[pltpu.VMEM((256, 256), BF16)] * 4, *[pltpu.VMEM((256, 128), BF16)] * 5,
            pltpu.VMEM((256, 640), BF16), pltpu.VMEM((256, 640), BF16), pltpu.VMEM((16, 256), BF16),
            pltpu.VMEM((256, 128), F32),
            *[pltpu.VMEM((256, 256), BF16)] * 3, pltpu.VMEM((512, 640), BF16), pltpu.VMEM((256, 256), F32),
            dma((9,)), *[dma((2, 3))] * 2, *[dma((2, 2, 4, 4))] * 2, *[dma((2, 8, 4))] * 2,
            *[dma((2, 2, 4))] * 2, *[dma((2, 2, 2, 8))] * 2, *[dma((2, 5, 8))] * 2, dma((4, 2)), dma((4, 2)), dma((2,)), dma((2,)),
        ],
        compiler_params=pltpu.CompilerParams(
            collective_id=0, has_side_effects=True, vmem_limit_bytes=60 * 1024 * 1024
        ),
        name="layer_step",
    )(
        entering_hidden.reshape(256, 128),
        aux,
        input_norm_gain.astype(F32).reshape(64, 128),
        query_matrix[0],
        key_matrix[0].T,
        value_matrix[0].T,
        output_matrix[0],
        adapter_down_maps[0, 0],
        adapter_up_query[0, 0],
        adapter_up_value[0, 0],
        rotated_key_cache.reshape(1536, 1024),
        cached_values.reshape(1536, 1024),
    )
    return out.reshape(1, 2, 2, 8192)


def solution(mesh):
    placed = (
        P(None, "wide", None), P(None, "wide", None), P(None, "wide"), P("segment", None),
        P("segment", None, "wide"), P("segment", None, "wide"), P("segment", None, "wide"), P("segment", None, "wide"),
        P("segment", "wide", None, None), P("segment", "wide", None, None), P("segment", "wide", None, None),
        P("segment", None, "wide", None, None), P("segment", None, "wide", None, None),
    )
    return jax.shard_map(
        on_device, mesh=mesh, in_specs=placed, out_specs=P("segment", None, "wide", None), check_vma=False
    )
```

```python
import jax
import jax.numpy as jnp
from jax import lax
from jax.experimental import pallas as pl
from jax.experimental.pallas import tpu as pltpu
from jax.sharding import PartitionSpec as P

HD = 128
RANK = 64
EPS = 1e-05
ROPE_BASE = 500000.0
ZS, XS, CS = 8, 4, 2
MESH = pl.DeviceIdType.MESH
F32 = jnp.float32
BF16 = jnp.bfloat16


def iota(shape, dim):
    return lax.broadcasted_iota(jnp.int32, shape, dim)


def onehot(cond):
    return jnp.where(cond, 1.0, 0.0).astype(BF16)


def dot(a, b):
    return jnp.dot(a, b, preferred_element_type=F32)


def dot_nt(a, b):
    return lax.dot_general(a, b, (((1,), (1,)), ((), ())), preferred_element_type=F32)


def kernel(
    h0_ref, aux_ref, gain_ref, wq_hbm, wk_hbm, wv_hbm, wo_hbm, down_hbm, upq_hbm, upv_hbm, kc_hbm, vc_hbm,
    out_ref,
    wq, wkv, wo, down, upq, upv, kc, vc,
    hst, tmp, hin, hres,
    xb1, xb2, fb1, fb2, xg, ag, acc_q, acc_kv, acc_d,
    ix_send, ix_mid, ix_recv, co_send, co_mid, co_swap, co_recv, qk_send, qk_mid, qk_swap, qk_recv, ou_send, ou_mid, ou_swap, ou_recv, ou_next,
    tq, tv, chosen, vmask, perm_a, perm_b, perm_c, perm_s, rows_q,
    wsem, xa_s, xa_r, za_s, za_r, ua_s, ua_r, zb_s, zb_r, xb_s, xb_r, ub_s, ub_r, asem_s, asem_r, hsem, nsem,
):
    seg = lax.axis_index("segment")
    me = lax.axis_index("wide")
    nseg = lax.axis_size("segment")
    z = me // (XS * CS)
    xc = me % (XS * CS)
    x = xc // CS
    c = xc % CS
    grp = z * CS + c

    def wide(zz, xx, cc):
        return {"wide": (zz * XS + xx) * CS + cc}

    def remote(src, dst, ssem, rsem, dev):
        return pltpu.make_async_remote_copy(
            src_ref=src, dst_ref=dst, send_sem=ssem, recv_sem=rsem, device_id=dev, device_id_type=MESH
        )

    loads = [
        pltpu.make_async_copy(wq_hbm, wq, wsem.at[0]),
        pltpu.make_async_copy(wk_hbm, wkv.at[pl.ds(0, 16)], wsem.at[1]),
        pltpu.make_async_copy(wv_hbm, wkv.at[pl.ds(16, 16)], wsem.at[2]),
        pltpu.make_async_copy(down_hbm, down, wsem.at[3]),
        pltpu.make_async_copy(upq_hbm, upq.at[pl.ds(0, RANK)], wsem.at[4]),
        pltpu.make_async_copy(upv_hbm, upv.at[pl.ds(RANK, RANK)], wsem.at[5]),
        pltpu.make_async_copy(kc_hbm, kc, wsem.at[6]),
        pltpu.make_async_copy(vc_hbm, vc, wsem.at[7]),
        pltpu.make_async_copy(wo_hbm, wo, wsem.at[8]),
    ]
    for load in loads:
        load.start()

    barrier = pltpu.get_barrier_semaphore()
    for k in range(1, 8):
        other = (xc + k) % 8
        pl.semaphore_signal(barrier, inc=1, device_id={"wide": z * 8 + other}, device_id_type=MESH)
        pl.semaphore_signal(barrier, inc=1, device_id={"wide": ((z + k) % 8) * 8 + xc}, device_id_type=MESH)

    for k in (1, nseg - 1):
        for other in range(8):
            pl.semaphore_signal(
                barrier, inc=1, device_id={"segment": (seg + k) % nseg, "wide": other * 8 + xc}, device_id_type=MESH
            )
    wkv[32:128, :] = jnp.zeros((96, wkv.shape[1]), BF16)
    upq[RANK:2 * RANK, :] = jnp.zeros((RANK, upq.shape[1]), BF16)
    upv[0:RANK, :] = jnp.zeros((RANK, upv.shape[1]), BF16)
    i, k = iota((256, 256), 0), iota((256, 256), 1)
    zi, xi, ri = (i >> 2) & 7, i >> 6, i & 3
    perm_a[...] = onehot(k == jnp.where((i & 32) == 0, zi * 16 + xi * 4, 128 + xi * 32 + zi * 4) + ri)
    perm_b[...] = onehot(k == zi * 32 + (i >> 5) * 4 + ri)
    perm_c[...] = onehot(k == (i & 63) * 4 + (i >> 6))
    i, k = iota((512, 640), 0), iota((512, 640), 1)
    perm_s[...] = onehot(k == ((i >> 3) & 7) * 80 + (i >> 6) * 8 + (i & 7))
    pl.semaphore_wait(barrier, 30)

    pending = []

    def stage_one(number, send, mid, rows):
        dest = mid.at[:, pl.ds(pl.multiple_of(xc * rows, rows), rows), :]
        pltpu.make_async_copy(send.at[xc], dest, asem_r.at[number, 0]).start()
        for k in range(1, 8):
            other = (xc + k) % 8
            remote(send.at[other], dest, asem_s.at[number, 0], asem_r.at[number, 0], {"wide": z * 8 + other}).start()

    def stage_two(number, mid, recv, rows):
        pltpu.make_async_copy(mid, mid, asem_r.at[number, 0]).wait()
        mine = pl.ds(pl.multiple_of(z * 8 * rows, 8 * rows), 8 * rows)
        pltpu.make_async_copy(mid.at[z], recv.at[mine], asem_r.at[number, 1]).start()
        for k in range(1, 8):
            other = (z + k) % 8
            remote(
                mid.at[other], recv.at[mine], asem_s.at[number, 1], asem_r.at[number, 1], {"wide": other * 8 + xc}
            ).start()

    for side, ref in enumerate((ix_send, ix_mid)):
        pending.append(
            lambda side=side, ref=ref: pltpu.make_async_copy(ref.at[pl.ds(0, 7)], ref.at[pl.ds(0, 7)], asem_s.at[0, side]).wait()
        )

    def in_plane(number, send, mid, count):
        def rows(n):
            return pl.ds(pl.multiple_of(n * count, 16), count)

        pltpu.make_async_copy(send.at[rows(xc)], mid.at[rows(xc)], asem_r.at[number, 0]).start()
        for k in range(1, 8):
            other = (xc + k) % 8
            remote(
                send.at[rows(other)], mid.at[rows(xc)], asem_s.at[number, 0], asem_r.at[number, 0], {"wide": z * 8 + other}
            ).start()

    def in_plane_done(number, mid):
        pltpu.make_async_copy(mid, mid, asem_r.at[number, 0]).wait()

    def along_line(number, swapped, recv, count):
        def rows(n):
            return pl.ds(pl.multiple_of(n * count, 16), count)

        pltpu.make_async_copy(swapped.at[rows(z)], recv.at[rows(z)], asem_r.at[number, 1]).start()
        for k in range(1, 8):
            other = (z + k) % 8
            remote(
                swapped.at[rows(other)], recv.at[rows(z)], asem_s.at[number, 1], asem_r.at[number, 1], {"wide": other * 8 + xc}
            ).start()

    def along_line_done(number, send, swapped, recv, count):
        pltpu.make_async_copy(recv, recv, asem_r.at[number, 1]).wait()
        part = pl.ds(0, 7 * count)
        pending.append(lambda: pltpu.make_async_copy(send.at[part], send.at[part], asem_s.at[number, 0]).wait())
        pending.append(lambda: pltpu.make_async_copy(swapped.at[part], swapped.at[part], asem_s.at[number, 1]).wait())

    def block_swap(tiles):
        block = iota((8, 128), 1) >> 4
        shifted = [[pltpu.roll(t, 16 * k, 1) if k else t for t in tiles] for k in range(8)]
        swapped = []
        for p in range(8):
            total = jnp.zeros((8, 128), F32)
            for k in range(8):
                total = jnp.where(block == (p + k) % 8, shifted[k][(p + k) % 8], total)
            swapped.append(jnp.concatenate([total, jnp.zeros((8, 128), F32)], axis=0).astype(BF16))
        return swapped

    def fold(dest, base):
        for m in range(16):
            dest[pl.ds(base, 16), m * 128:(m + 1) * 128] = tmp[pl.ds(m, 16, stride=16), :].astype(BF16)

    def unfold(source, base, dest, to):
        i, k = iota((64, 64), 0), iota((64, 64), 1)
        perm = onehot(k == ((i >> 2) & 3) * 16 + (i & 3) * 4 + (i >> 4))
        for part in range(4):
            moved = dot(perm, source[pl.ds(base, 64), part * 512:(part + 1) * 512]).astype(BF16)
            for q in range(4):
                dest[pl.ds(to, 16), q * 2048 + part * 512:q * 2048 + (part + 1) * 512] = moved[16 * q:16 * q + 16]

    ends = {0: [], 1: []}

    def gather(number, xb, fb, full, meanwhile=lambda: None):
        partner = wide(z, x, 1 - c)

        def block(xo, zo, half=None):
            at = pl.multiple_of((((x + xo) % XS) * ZS + (z + zo) % ZS) * 16, 16)
            return fb.at[pl.ds(at, 16), pl.ds(0, 2048) if half is None else pl.ds(half * 1024, 1024)]

        def chunk(zo, q):
            at = pl.multiple_of(((z + zo) % ZS) * 16, 16)
            return full.at[pl.ds(at, 16), pl.ds(q * 2048, 2048)]

        def share_a(zo, q):
            s = number, zo % ZS, q
            return remote(chunk(zo, q), chunk(zo, q), ua_s.at[s], ua_r.at[s], partner)

        def share_b(kind, zo):
            s = number, kind, zo % ZS
            at = block((0, 3, 1, 2, 2)[kind], zo, (None, None, None, 0, 1)[kind])
            return remote(at, at, ub_s.at[s], ub_r.at[s], partner)

        def spread(xo):
            for zh in range(2):
                xx = (x + xo) % XS
                unfold(
                    fb, pl.multiple_of((xx * ZS + zh * 4) * 16, 64), full, pl.multiple_of(128 + xx * 32 + zh * 16, 16)
                )

        @pl.when(c == 0)
        def _():
            sent = ends[0]

            def go(make, *args):
                make(*args).start()
                sent.append(lambda: make(*args).wait_send())

            def hop(k):
                own = xb.at[pl.ds(pl.multiple_of(x * 16, 16), 16)]
                return remote(own, own, xa_s.at[number, k - 1], xa_r.at[number, k - 1], wide(z, (x + k) % XS, c))

            fold(xb, pl.multiple_of(x * 16, 16))
            for k in range(1, XS):
                go(hop, k)
            for k in range(1, XS):
                hop(k).wait_recv()
            unfold(xb, 0, full, pl.multiple_of(z * 16, 16))

            def ring(direction, step, q):
                at = chunk(-step if direction == 0 else step, q)
                s = number, direction, step, q
                target = (z + (1 if direction == 0 else ZS - 1)) % ZS
                return remote(at, at, za_s.at[s], za_r.at[s], wide(target, x, c))

            def landed(direction, step, q):
                at = chunk(-(step + 1) if direction == 0 else step + 1, q)
                s = number, direction, step, q
                remote(at, at, za_s.at[s], za_r.at[s], partner).wait_recv()

            for q in range(4):
                for direction in range(2):
                    go(ring, direction, 0, q)
            for q in range(4):
                go(share_a, 0, q)
            meanwhile()
            for step in range(3):
                for q in range(4):
                    for direction in range(2):
                        landed(direction, step, q)
                        if step < 2 or q // 2 == direction:
                            go(ring, direction, step + 1, q)
                        go(share_a, -(step + 1) if direction == 0 else step + 1, q)
            for kinds, xo in (((0,), 0), ((1,), 3), ((2,), 1), ((3, 4), 2)):
                if xo == 2:
                    for q in range(2):
                        for direction in range(2):
                            landed(direction, 3, 2 * direction + q)
                            go(share_a, 4, 2 * direction + q)
                for zo in range(ZS):
                    for kind in kinds:
                        share_b(kind, zo).wait_recv()
                spread(xo)

        @pl.when(c == 1)
        def _():
            sent = ends[1]

            def go(make, *args):
                make(*args).start()
                sent.append(lambda: make(*args).wait_send())

            def along_z(direction, step, half=None):
                at = block(0, -step if direction == 0 else step, half)
                s = number, direction, step
                target = (z + (1 if direction == 0 else ZS - 1)) % ZS
                return remote(at, at, zb_s.at[s], zb_r.at[s], wide(target, x, c))

            def from_z(direction, step, half=None):
                at = block(0, -(step + 1) if direction == 0 else step + 1, half)
                s = number, direction, step
                remote(at, at, zb_s.at[s], zb_r.at[s], partner).wait_recv()

            def along_x(direction, step, zo):
                at = block(0, zo) if step == 0 else block(3 if direction == 0 else 1, zo, direction)
                s = number, direction, step, zo % ZS
                target = (x + (1 if direction == 0 else XS - 1)) % XS
                return remote(at, at, xb_s.at[s], xb_r.at[s], wide(z, target, c))

            def from_x(direction, step, zo):
                at = block(3 if direction == 0 else 1, zo) if step == 0 else block(2, zo, direction)
                s = number, direction, step, zo % ZS
                remote(at, at, xb_s.at[s], xb_r.at[s], partner).wait_recv()

            def have(zo):
                go(along_x, 0, 0, zo)
                go(along_x, 1, 0, zo)
                go(share_b, 0, zo)

            def relay(zo):
                for direction in range(2):
                    from_x(direction, 0, zo)
                    go(along_x, direction, 1, zo)
                    go(share_b, 1 + direction, zo)

            fold(fb, pl.multiple_of((x * ZS + z) * 16, 16))
            go(along_z, 0, 0)
            go(along_z, 1, 0)
            have(0)
            for step in range(3):
                for direction in range(2):
                    from_z(direction, step)
                    go(along_z, direction, step + 1, None if step < 2 else direction)
                    have(-(step + 1) if direction == 0 else step + 1)
                if step == 0:
                    relay(0)
                    meanwhile()
                else:
                    relay(-step)
                    relay(step)
            from_z(0, 3, 0)
            from_z(1, 3, 1)
            have(4)
            relay(-3)
            relay(3)
            spread(0)
            relay(4)
            spread(3)
            spread(1)
            for zo in (0, 7, 1, 6, 2, 5, 3, 4):
                for direction in range(2):
                    from_x(direction, 1, zo)
                    go(share_b, 3 + direction, zo)
            spread(2)
            for zo in range(ZS):
                for q in range(4):
                    share_a(zo, q).wait_recv()

    ix = jnp.broadcast_to(aux_ref[16:24, :][None], (8, 8, 128))
    for i in range(8):
        ix_send[i] = ix
    stage_one(0, ix_send, ix_mid, 8)

    def prepare():
        pltpu.make_async_copy(ix_recv, ix_recv, asem_r.at[0, 1]).wait()
        i, k = iota((256, 512), 0), iota((256, 512), 1)
        first = (((i >> 4) & 7) * XS + ((i >> 2) & 3)) * CS
        second = (((i >> 2) & 7) * XS + ((i >> 5) & 3)) * CS + 1
        source = jnp.where(i < 128, first, second) * 8 + (i & 3)
        names = dot(onehot(k == source), ix_recv[...].astype(BF16))
        row = names.T
        same = jnp.broadcast_to(names[:, 0:1], (256, 256)) == jnp.broadcast_to(row[0:1, :], (256, 256))
        before = same & (iota((256, 256), 1) < iota((256, 256), 0))
        order = jnp.sum(jnp.where(before, 1.0, 0.0), axis=1, keepdims=True)
        name = names[:, 0:1].astype(jnp.int32)
        at = (name >> 3) * 80 + order.astype(jnp.int32)
        spots = iota((256, 640), 1)
        tq[...] = onehot(spots == at + (name & 7) * 8)
        tv[...] = onehot(spots == at + 64)
        vmask[...] = jnp.where((iota((256, 128), 1) >> 4) == (names.astype(jnp.int32) & 7), 1.0, 0.0)
        order_row = jnp.broadcast_to(order, (256, 128)).T
        mine = (row[0:16, :].astype(jnp.int32) == me) & (order_row[0:16, :].astype(jnp.int32) == iota((16, 256), 0))
        chosen[...] = onehot(mine)

    def passing():
        return remote(hres, hin, hsem.at[0], hsem.at[1], {"segment": (seg + 1) % nseg})

    @pl.when(seg == 0)
    def _():
        hres[...] = h0_ref[...]
        hst[...] = h0_ref[...].astype(F32)

    @pl.when(seg > 0)
    def _():
        stage_two(0, ix_mid, ix_recv, 8)
        prepare()
        passing().wait_recv()
        pltpu.make_async_copy(ou_next, ou_next, nsem.at[1]).wait()
        for r in range(4):
            rows = slice(r * 64, (r + 1) * 64)
            result = (hin[rows, :].astype(F32) + dot(perm_c[rows, :], ou_next[...])).astype(BF16)
            hres[rows, :] = result
            hst[rows, :] = result.astype(F32)

    gain = gain_ref[...]
    for r in range(4):
        block = hst[r * 64:(r + 1) * 64, :]
        total = jnp.sum(jnp.sum(block * block, axis=1, keepdims=True), axis=0, keepdims=True)
        tmp[r * 64:(r + 1) * 64, :] = block * lax.rsqrt(total * (1.0 / 8192.0) + EPS) * gain

    @pl.when(seg < nseg - 1)
    def _():
        passing().start()

    def meanwhile():
        @pl.when(seg == 0)
        def _():
            stage_two(0, ix_mid, ix_recv, 8)

    gather(0, xb1, fb1, xg, meanwhile)


    for n in range(6):
        loads[n].wait()
    acc_q[...] = jnp.zeros_like(acc_q)
    acc_kv[...] = jnp.zeros_like(acc_kv)
    acc_d[...] = jnp.zeros_like(acc_d)

    def column(n):
        return pl.ds(pl.multiple_of(n * 1024, 1024), 1024)

    @pl.loop(0, 8)
    def _(n):
        acc_d[...] += dot(xg[:, column(n)], down[column(n), :])

    @pl.when(seg == 0)
    def _():
        prepare()

    low = dot(chosen[...], acc_d[...].astype(BF16)).astype(BF16)
    values = []
    for part in range(0, 8, 2):
        q_slots = [dot(low, upq[:, (part + n) * 1024:(part + n + 1) * 1024])[0:8] for n in range(2)]
        values += [dot(low, upv[:, (part + n) * 128:(part + n + 1) * 128])[0:8] for n in range(2)]
        for n in range(8):
            tile = jnp.concatenate([q[:, n * 128:(n + 1) * 128] for q in q_slots], axis=0)
            co_send[n * 80 + part * 8:n * 80 + part * 8 + 16, :] = tile.astype(BF16)
    for n, tile in enumerate(block_swap(values)):
        co_send[n * 80 + 64:n * 80 + 80, :] = tile
    in_plane(1, co_send, co_mid, 80)

    @pl.loop(0, 8)
    def _(n):
        acc_q[...] += dot(xg[:, column(n)], wq[column(n), :])

    in_plane_done(1, co_mid)
    swapped = dot(perm_s[...], co_mid[...]).astype(BF16)
    values = [co_mid[n * 80 + 64:n * 80 + 80, :].astype(F32)[0:8] for n in range(8)]
    for n, tile in enumerate(block_swap(values)):
        co_swap[n * 80:n * 80 + 64, :] = swapped[n * 64:(n + 1) * 64]
        co_swap[n * 80 + 64:n * 80 + 80, :] = tile
    along_line(1, co_swap, co_recv, 80)

    @pl.loop(0, 8)
    def _(n):
        acc_kv[...] += dot_nt(xg[:, column(n)], wkv[:, column(n)])

    along_line_done(1, co_send, co_swap, co_recv, 80)

    a, b = iota((128, 128), 0), iota((128, 128), 1)
    moved = co_recv[...]
    query = acc_q[...] + 0.5 * dot(tq[...], moved)
    narrow = onehot((b >= 16) & (b < 32) & ((a & 15) == b - 16))
    fresh = acc_kv[...] + 0.5 * dot((dot(tv[...], moved) * vmask[...]).astype(BF16), narrow)
    qk_send[...] = dot(perm_a[...], jnp.concatenate([query.astype(BF16), fresh.astype(BF16)], axis=1)).astype(BF16)
    in_plane(2, qk_send, qk_mid, 32)
    in_plane_done(2, qk_mid)
    qk_swap[...] = dot(perm_b[...], qk_mid[...]).astype(BF16)
    along_line(2, qk_swap, qk_recv, 32)
    along_line_done(2, qk_send, qk_swap, qk_recv, 32)
    rows_q[...] = dot(perm_c[...], qk_recv[...])

    loads[6].wait()
    loads[7].wait()
    spread_k = onehot(a == (b & 15))
    spread_v = onehot(a == (b & 15) + 16)
    a, b = iota((64, 128), 0), iota((64, 128), 1)
    lanes = (b >> 4) == (a & 7)
    a, b = iota((64, 64), 0), iota((64, 64), 1)
    heads = onehot((a >> 3) == (b >> 3))
    a, b = iota((64, 1024), 0), iota((64, 1024), 1)
    diagonal = (b >> 7) == (a >> 3)
    past = iota((64, 384), 1)
    scale = HD ** (-0.5)
    for r in range(4):
        cosine, sine = aux_ref[r:r + 1, :], aux_ref[4 + r:5 + r, :]
        length = aux_ref[8 + r:9 + r, 0:1].astype(jnp.int32)
        q_row = rows_q[r * 64:(r + 1) * 64, 0:128]
        kv_row = rows_q[r * 64:(r + 1) * 64, 128:256].astype(BF16)
        k_row = dot(heads, jnp.where(lanes, dot(kv_row, spread_k), 0.0).astype(BF16))
        v_row = dot(heads, jnp.where(lanes, dot(kv_row, spread_v), 0.0).astype(BF16))
        q_rot = (q_row * cosine + pltpu.roll(q_row, 64, 1) * sine).astype(BF16).astype(F32)
        k_rot = (k_row * cosine + pltpu.roll(k_row, 64, 1) * sine).astype(BF16).astype(F32)
        own = jnp.sum(q_rot * k_rot, axis=1, keepdims=True) * scale
        wide_q = jnp.where(diagonal, jnp.concatenate([q_rot] * 8, axis=1), 0.0).astype(BF16)
        scores = dot_nt(wide_q, kc[r * 384:(r + 1) * 384, :]) * scale
        valid = past < length
        scores = jnp.where(valid, scores, -1e30)
        top = jnp.maximum(jnp.max(scores, axis=1, keepdims=True), own)
        powers = jnp.where(valid, jnp.exp(scores - top), 0.0)
        own_power = jnp.exp(own - top)
        total = jnp.sum(powers, axis=1, keepdims=True) + own_power
        weights = (powers / total).astype(BF16)
        own_weight = (own_power / total).astype(BF16).astype(F32)
        mixed = dot(weights, vc[r * 384:(r + 1) * 384, :])
        mixed = jnp.concatenate([mixed[8 * g:8 * g + 8, 128 * g:128 * g + 128] for g in range(8)], axis=0)
        tmp[r * 64:(r + 1) * 64, :] = mixed + own_weight * v_row

    gather(1, xb2, fb2, ag)

    loads[8].wait()
    acc_q[...] = jnp.zeros_like(acc_q)

    @pl.loop(0, 8)
    def _(n):
        part = pl.ds(pl.multiple_of(n * 1024, 1024), 1024)
        acc_q[...] += dot(ag[:, part], wo[part, :])

    ou_send[...] = dot(perm_a[...], acc_q[...].astype(BF16)).astype(BF16)
    in_plane(3, ou_send, ou_mid, 32)
    in_plane_done(3, ou_mid)
    ou_swap[...] = dot(perm_b[...], ou_mid[...]).astype(BF16)

    @pl.when(seg < nseg - 1)
    def _():
        for k in range(8):
            other = (z + k) % 8
            remote(
                ou_swap.at[pl.ds(pl.multiple_of(other * 32, 32), 32)], ou_next.at[pl.ds(pl.multiple_of(z * 32, 32), 32)],
                nsem.at[0], nsem.at[1], {"segment": seg + 1, "wide": other * 8 + xc},
            ).start()

    along_line(3, ou_swap, ou_recv, 32)
    along_line_done(3, ou_send, ou_swap, ou_recv, 32)
    for r in range(4):
        rows = slice(r * 64, (r + 1) * 64)
        out_ref[rows, :] = (hst[rows, :] + dot(perm_c[rows, :], ou_recv[...])).astype(BF16)

    @pl.when(seg < nseg - 1)
    def _():
        passing().wait_send()
        pltpu.make_async_copy(ou_swap, ou_swap, nsem.at[0]).wait()

    for wait in pending:
        wait()
    for core in range(CS):
        @pl.when(c == core)
        def _(core=core):
            for wait in ends[core]:
                wait()


def on_device(
    entering_hidden, row_adapter_index, lengths, input_norm_gain, query_matrix, key_matrix, value_matrix,
    output_matrix, adapter_down_maps, adapter_up_query, adapter_up_value, rotated_key_cache, cached_values,
):
    half = HD // 2
    positions = lengths.reshape(4, 1).astype(F32)
    inverse = ROPE_BASE ** (-jnp.arange(half, dtype=F32) / half)
    angles = positions * inverse[None, :]
    cosine, sine = jnp.cos(angles), jnp.sin(angles)
    spread = lambda v: jnp.pad(jnp.broadcast_to(v, (4, 128)), ((0, 4), (0, 0)))
    aux = jnp.concatenate(
        [
            jnp.concatenate([cosine, cosine], 1),
            jnp.concatenate([-sine, sine], 1),
            spread(positions),
            spread(row_adapter_index.reshape(4, 1).astype(F32)),
        ],
        0,
    )
    vmem = pl.BlockSpec(memory_space=pltpu.VMEM)
    hbm = pl.BlockSpec(memory_space=pl.ANY)
    tiles = lambda rows, kind: [
        pltpu.VMEM((8, 8, rows, 128), kind), pltpu.VMEM((8, 8 * rows, 128), kind), pltpu.VMEM((64 * rows, 128), kind)
    ]
    dma = pltpu.SemaphoreType.DMA
    out = pl.pallas_call(
        kernel,
        out_shape=jax.ShapeDtypeStruct((256, 128), BF16),
        in_specs=[vmem] * 3 + [hbm] * 9,
        out_specs=vmem,
        scratch_shapes=[
            pltpu.VMEM((8192, 128), BF16), pltpu.VMEM((128, 8192), BF16), pltpu.VMEM((8192, 128), BF16),
            pltpu.VMEM((8192, 128), BF16), pltpu.VMEM((128, 8192), BF16), pltpu.VMEM((128, 1024), BF16),
            pltpu.VMEM((1536, 1024), BF16), pltpu.VMEM((1536, 1024), BF16),
            pltpu.VMEM((256, 128), F32), pltpu.VMEM((256, 128), F32),
            pltpu.VMEM((256, 128), BF16), pltpu.VMEM((256, 128), BF16),
            pltpu.VMEM((64, 2048), BF16), pltpu.VMEM((64, 2048), BF16),
            pltpu.VMEM((512, 2048), BF16), pltpu.VMEM((512, 2048), BF16),
            pltpu.VMEM((256, 8192), BF16), pltpu.VMEM((256, 8192), BF16),
            pltpu.VMEM((256, 128), F32), pltpu.VMEM((256, 128), F32), pltpu.VMEM((256, 128), F32),
            *tiles(8, F32), *[pltpu.VMEM((640, 128), BF16)] * 4,
            *[pltpu.VMEM((256, 256), BF16)] * 4, *[pltpu.VMEM((256, 128), BF16)] * 5,
            pltpu.VMEM((256, 640), BF16), pltpu.VMEM((256, 640), BF16), pltpu.VMEM((16, 256), BF16),
            pltpu.VMEM((256, 128), F32),
            *[pltpu.VMEM((256, 256), BF16)] * 3, pltpu.VMEM((512, 640), BF16), pltpu.VMEM((256, 256), F32),
            dma((9,)), *[dma((2, 3))] * 2, *[dma((2, 2, 4, 4))] * 2, *[dma((2, 8, 4))] * 2,
            *[dma((2, 2, 4))] * 2, *[dma((2, 2, 2, 8))] * 2, *[dma((2, 5, 8))] * 2, dma((4, 2)), dma((4, 2)), dma((2,)), dma((2,)),
        ],
        compiler_params=pltpu.CompilerParams(
            collective_id=0, has_side_effects=True, vmem_limit_bytes=60 * 1024 * 1024
        ),
        name="layer_step",
    )(
        entering_hidden.reshape(256, 128),
        aux,
        input_norm_gain.astype(F32).reshape(64, 128),
        query_matrix[0],
        key_matrix[0].T,
        value_matrix[0].T,
        output_matrix[0],
        adapter_down_maps[0, 0],
        adapter_up_query[0, 0],
        adapter_up_value[0, 0],
        rotated_key_cache.reshape(1536, 1024),
        cached_values.reshape(1536, 1024),
    )
    return out.reshape(1, 2, 2, 8192)


def solution(mesh):
    placed = (
        P(None, "wide", None), P(None, "wide", None), P(None, "wide"), P("segment", None),
        P("segment", None, "wide"), P("segment", None, "wide"), P("segment", None, "wide"), P("segment", None, "wide"),
        P("segment", "wide", None, None), P("segment", "wide", None, None), P("segment", "wide", None, None),
        P("segment", None, "wide", None, None), P("segment", None, "wide", None, None),
    )
    return jax.shard_map(
        on_device, mesh=mesh, in_specs=placed, out_specs=P("segment", None, "wide", None), check_vma=False
    )
```

```python
import jax
import jax.numpy as jnp
from jax import lax
from jax.experimental import pallas as pl
from jax.experimental.pallas import tpu as pltpu
from jax.sharding import PartitionSpec as P

HD = 128
RANK = 64
EPS = 1e-05
ROPE_BASE = 500000.0
ZS, XS, CS = 8, 4, 2
MESH = pl.DeviceIdType.MESH
F32 = jnp.float32
BF16 = jnp.bfloat16


def iota(shape, dim):
    return lax.broadcasted_iota(jnp.int32, shape, dim)


def onehot(cond):
    return jnp.where(cond, 1.0, 0.0).astype(BF16)


def dot(a, b):
    return jnp.dot(a, b, preferred_element_type=F32)


def dot_nt(a, b):
    return lax.dot_general(a, b, (((1,), (1,)), ((), ())), preferred_element_type=F32)


def kernel(
    h0_ref, aux_ref, gain_ref, wq_hbm, wk_hbm, wv_hbm, wo_hbm, down_hbm, upq_hbm, upv_hbm, kc_hbm, vc_hbm,
    out_ref,
    wq, wkv, wo, down, upq, upv, kc, vc,
    hst, tmp, hin, hres,
    fa1, fa2, fb1, fb2, xg, ag, acc_q, acc_kv, acc_d,
    ix_send, ix_mid, ix_recv, co_send, co_mid, co_swap, co_recv, qk_send, qk_mid, qk_swap, qk_recv, ou_send, ou_mid, ou_swap, ou_recv, ou_next,
    tq, tv, chosen, vmask, perm_a, perm_b, perm_c, perm_s, rows_q,
    wsem, xa_s, xa_r, za_s, za_r, ua_s, ua_r, zb_s, zb_r, xb_s, xb_r, ub_s, ub_r, asem_s, asem_r, hsem, nsem,
):
    seg = lax.axis_index("segment")
    me = lax.axis_index("wide")
    nseg = lax.axis_size("segment")
    z = me // (XS * CS)
    xc = me % (XS * CS)
    x = xc // CS
    c = xc % CS
    grp = z * CS + c

    def wide(zz, xx, cc):
        return {"wide": (zz * XS + xx) * CS + cc}

    def remote(src, dst, ssem, rsem, dev):
        return pltpu.make_async_remote_copy(
            src_ref=src, dst_ref=dst, send_sem=ssem, recv_sem=rsem, device_id=dev, device_id_type=MESH
        )

    loads = [
        pltpu.make_async_copy(wq_hbm, wq, wsem.at[0]),
        pltpu.make_async_copy(wk_hbm, wkv.at[pl.ds(0, 16)], wsem.at[1]),
        pltpu.make_async_copy(wv_hbm, wkv.at[pl.ds(16, 16)], wsem.at[2]),
        pltpu.make_async_copy(down_hbm, down, wsem.at[3]),
        pltpu.make_async_copy(upq_hbm, upq.at[pl.ds(0, RANK)], wsem.at[4]),
        pltpu.make_async_copy(upv_hbm, upv.at[pl.ds(RANK, RANK)], wsem.at[5]),
        pltpu.make_async_copy(kc_hbm, kc, wsem.at[6]),
        pltpu.make_async_copy(vc_hbm, vc, wsem.at[7]),
        pltpu.make_async_copy(wo_hbm, wo, wsem.at[8]),
    ]
    for load in loads:
        load.start()

    barrier = pltpu.get_barrier_semaphore()
    for k in range(1, 8):
        other = (xc + k) % 8
        pl.semaphore_signal(barrier, inc=1, device_id={"wide": z * 8 + other}, device_id_type=MESH)
        pl.semaphore_signal(barrier, inc=1, device_id={"wide": ((z + k) % 8) * 8 + xc}, device_id_type=MESH)

    for k in (1, nseg - 1):
        for other in range(8):
            pl.semaphore_signal(
                barrier, inc=1, device_id={"segment": (seg + k) % nseg, "wide": other * 8 + xc}, device_id_type=MESH
            )
    wkv[32:128, :] = jnp.zeros((96, wkv.shape[1]), BF16)
    upq[RANK:2 * RANK, :] = jnp.zeros((RANK, upq.shape[1]), BF16)
    upv[0:RANK, :] = jnp.zeros((RANK, upv.shape[1]), BF16)
    i, k = iota((256, 256), 0), iota((256, 256), 1)
    zi, xi, ri = (i >> 2) & 7, i >> 6, i & 3
    perm_a[...] = onehot(k == jnp.where((i & 32) == 0, zi * 16 + xi * 4, 128 + xi * 32 + zi * 4) + ri)
    perm_b[...] = onehot(k == zi * 32 + (i >> 5) * 4 + ri)
    perm_c[...] = onehot(k == (i & 63) * 4 + (i >> 6))
    i, k = iota((512, 640), 0), iota((512, 640), 1)
    perm_s[...] = onehot(k == ((i >> 3) & 7) * 80 + (i >> 6) * 8 + (i & 7))
    pl.semaphore_wait(barrier, 30)

    pending = []

    def stage_one(number, send, mid, rows):
        dest = mid.at[:, pl.ds(pl.multiple_of(xc * rows, rows), rows), :]
        pltpu.make_async_copy(send.at[xc], dest, asem_r.at[number, 0]).start()
        for k in range(1, 8):
            other = (xc + k) % 8
            remote(send.at[other], dest, asem_s.at[number, 0], asem_r.at[number, 0], {"wide": z * 8 + other}).start()

    def stage_two(number, mid, recv, rows):
        pltpu.make_async_copy(mid, mid, asem_r.at[number, 0]).wait()
        mine = pl.ds(pl.multiple_of(z * 8 * rows, 8 * rows), 8 * rows)
        pltpu.make_async_copy(mid.at[z], recv.at[mine], asem_r.at[number, 1]).start()
        for k in range(1, 8):
            other = (z + k) % 8
            remote(
                mid.at[other], recv.at[mine], asem_s.at[number, 1], asem_r.at[number, 1], {"wide": other * 8 + xc}
            ).start()

    for side, ref in enumerate((ix_send, ix_mid)):
        pending.append(
            lambda side=side, ref=ref: pltpu.make_async_copy(ref.at[pl.ds(0, 7)], ref.at[pl.ds(0, 7)], asem_s.at[0, side]).wait()
        )

    def in_plane(number, send, mid, count):
        def rows(n):
            return pl.ds(pl.multiple_of(n * count, 16), count)

        pltpu.make_async_copy(send.at[rows(xc)], mid.at[rows(xc)], asem_r.at[number, 0]).start()
        for k in range(1, 8):
            other = (xc + k) % 8
            remote(
                send.at[rows(other)], mid.at[rows(xc)], asem_s.at[number, 0], asem_r.at[number, 0], {"wide": z * 8 + other}
            ).start()

    def in_plane_done(number, mid):
        pltpu.make_async_copy(mid, mid, asem_r.at[number, 0]).wait()

    def along_line(number, swapped, recv, count):
        def rows(n):
            return pl.ds(pl.multiple_of(n * count, 16), count)

        pltpu.make_async_copy(swapped.at[rows(z)], recv.at[rows(z)], asem_r.at[number, 1]).start()
        for k in range(1, 8):
            other = (z + k) % 8
            remote(
                swapped.at[rows(other)], recv.at[rows(z)], asem_s.at[number, 1], asem_r.at[number, 1], {"wide": other * 8 + xc}
            ).start()

    def along_line_done(number, send, swapped, recv, count):
        pltpu.make_async_copy(recv, recv, asem_r.at[number, 1]).wait()
        part = pl.ds(0, 7 * count)
        pending.append(lambda: pltpu.make_async_copy(send.at[part], send.at[part], asem_s.at[number, 0]).wait())
        pending.append(lambda: pltpu.make_async_copy(swapped.at[part], swapped.at[part], asem_s.at[number, 1]).wait())

    def block_swap(tiles):
        block = iota((8, 128), 1) >> 4
        shifted = [[pltpu.roll(t, 16 * k, 1) if k else t for t in tiles] for k in range(8)]
        swapped = []
        for p in range(8):
            total = jnp.zeros((8, 128), F32)
            for k in range(8):
                total = jnp.where(block == (p + k) % 8, shifted[k][(p + k) % 8], total)
            swapped.append(jnp.concatenate([total, jnp.zeros((8, 128), F32)], axis=0).astype(BF16))
        return swapped

    def fold(dest, base):
        for m in range(16):
            dest[pl.ds(base, 16), m * 128:(m + 1) * 128] = tmp[pl.ds(m, 16, stride=16), :].astype(BF16)

    def unfold(source, base, dest, to):
        i, k = iota((64, 64), 0), iota((64, 64), 1)
        perm = onehot(k == ((i >> 2) & 3) * 16 + (i & 3) * 4 + (i >> 4))
        for part in range(4):
            moved = dot(perm, source[pl.ds(base, 64), part * 512:(part + 1) * 512]).astype(BF16)
            for q in range(4):
                dest[pl.ds(to, 16), q * 2048 + part * 512:q * 2048 + (part + 1) * 512] = moved[16 * q:16 * q + 16]

    ends = {0: [], 1: []}

    def gather(number, fa, fb, full, meanwhile=lambda: None):
        partner = wide(z, x, 1 - c)

        def block(xo, zo, half=None):
            at = pl.multiple_of((((x + xo) % XS) * ZS + (z + zo) % ZS) * 16, 16)
            return fb.at[pl.ds(at, 16), pl.ds(0, 2048) if half is None else pl.ds(half * 1024, 1024)]

        def block_a(xo, zo, half=None):
            at = pl.multiple_of((((z + zo) % ZS) * XS + (x + xo) % XS) * 16, 16)
            return fa.at[pl.ds(at, 16), pl.ds(0, 2048) if half is None else pl.ds(half * 1024, 1024)]

        def share_a(xo, zo, half=None):
            s = number, xo, 8 if half == 1 else zo % ZS
            at = block_a(xo, zo, half)
            return remote(at, at, ua_s.at[s], ua_r.at[s], partner)

        def share_b(kind, zo):
            s = number, kind, zo % ZS
            at = block((0, 3, 1, 2, 2)[kind], zo, (None, None, None, 0, 1)[kind])
            return remote(at, at, ub_s.at[s], ub_r.at[s], partner)

        def spread(xo):
            for zh in range(2):
                xx = (x + xo) % XS
                unfold(
                    fb, pl.multiple_of((xx * ZS + zh * 4) * 16, 64), full, pl.multiple_of(128 + xx * 32 + zh * 16, 16)
                )

        def level(zo, wait):
            if wait:
                for xo in range(XS):
                    for half in (0, 1) if zo == 4 else (None,):
                        share_a(xo, zo, half).wait_recv()
            zz = (z + zo) % ZS
            unfold(fa, pl.multiple_of(zz * 64, 64), full, pl.multiple_of(zz * 16, 16))

        @pl.when(c == 0)
        def _():
            sent = ends[0]

            def go(make, *args):
                make(*args).start()
                sent.append(lambda: make(*args).wait_send())

            def hop(k, offset=0):
                at = block_a(offset, 0)
                return remote(at, at, xa_s.at[number, k - 1], xa_r.at[number, k - 1], wide(z, (x + k) % XS, c))

            def ring(direction, step, xo, half=None):
                at = block_a(xo, -step if direction == 0 else step, half)
                s = number, direction, step, xo
                target = (z + (1 if direction == 0 else ZS - 1)) % ZS
                return remote(at, at, za_s.at[s], za_r.at[s], wide(target, x, c))

            def landed(direction, step, xo, half=None):
                at = block_a(xo, -(step + 1) if direction == 0 else step + 1, half)
                s = number, direction, step, xo
                remote(at, at, za_s.at[s], za_r.at[s], partner).wait_recv()

            def enter(xo):
                go(ring, 0, 0, xo)
                go(ring, 1, 0, xo)
                go(share_a, xo, 0)

            def onward(step, xo):
                for direction in range(2):
                    landed(direction, step, xo)
                    go(ring, direction, step + 1, xo, None if step < 2 else direction)
                    go(share_a, xo, -(step + 1) if direction == 0 else step + 1)

            fold(fa, pl.multiple_of((z * XS + x) * 16, 16))
            for k in (1, 3, 2):
                go(hop, k)
            enter(0)
            for k in (1, 3):
                hop(k, XS - k).wait_recv()
                enter(XS - k)
            onward(0, 0)
            hop(2, 2).wait_recv()
            enter(2)
            level(0, False)
            for xo in (3, 1, 2):
                onward(0, xo)
            meanwhile()
            for step in (1, 2):
                level(-step, False)
                level(step, False)
                for xo in (0, 3, 1, 2):
                    onward(step, xo)
            level(-3, False)
            level(3, False)
            for kinds, xo in (((0,), 0), ((1,), 3), ((2,), 1), ((3, 4), 2)):
                if xo == 2:
                    for xq in (0, 3, 1, 2):
                        for direction in range(2):
                            landed(direction, 3, xq, direction)
                            go(share_a, xq, 4, direction)
                    level(4, False)
                for zo in range(ZS):
                    for kind in kinds:
                        share_b(kind, zo).wait_recv()
                spread(xo)

        @pl.when(c == 1)
        def _():
            sent = ends[1]

            def go(make, *args):
                make(*args).start()
                sent.append(lambda: make(*args).wait_send())

            def along_z(direction, step, half=None):
                at = block(0, -step if direction == 0 else step, half)
                s = number, direction, step
                target = (z + (1 if direction == 0 else ZS - 1)) % ZS
                return remote(at, at, zb_s.at[s], zb_r.at[s], wide(target, x, c))

            def from_z(direction, step, half=None):
                at = block(0, -(step + 1) if direction == 0 else step + 1, half)
                s = number, direction, step
                remote(at, at, zb_s.at[s], zb_r.at[s], partner).wait_recv()

            def along_x(direction, step, zo):
                at = block(0, zo) if step == 0 else block(3 if direction == 0 else 1, zo, direction)
                s = number, direction, step, zo % ZS
                target = (x + (1 if direction == 0 else XS - 1)) % XS
                return remote(at, at, xb_s.at[s], xb_r.at[s], wide(z, target, c))

            def from_x(direction, step, zo):
                at = block(3 if direction == 0 else 1, zo) if step == 0 else block(2, zo, direction)
                s = number, direction, step, zo % ZS
                remote(at, at, xb_s.at[s], xb_r.at[s], partner).wait_recv()

            def have(zo):
                go(along_x, 0, 0, zo)
                go(along_x, 1, 0, zo)
                go(share_b, 0, zo)

            def relay(zo):
                for direction in range(2):
                    from_x(direction, 0, zo)
                    go(along_x, direction, 1, zo)
                    go(share_b, 1 + direction, zo)

            fold(fb, pl.multiple_of((x * ZS + z) * 16, 16))
            go(along_z, 0, 0)
            go(along_z, 1, 0)
            have(0)
            for step in range(3):
                for direction in range(2):
                    from_z(direction, step)
                    go(along_z, direction, step + 1, None if step < 2 else direction)
                    have(-(step + 1) if direction == 0 else step + 1)
                if step == 0:
                    relay(0)
                    meanwhile()
                else:
                    relay(-step)
                    relay(step)
            from_z(0, 3, 0)
            from_z(1, 3, 1)
            have(4)
            relay(-3)
            relay(3)
            level(0, True)
            spread(0)
            relay(4)
            level(-1, True)
            level(1, True)
            spread(3)
            spread(1)
            level(-2, True)
            level(2, True)
            for zo in (0, 7, 1, 6, 2, 5, 3, 4):
                for direction in range(2):
                    from_x(direction, 1, zo)
                    go(share_b, 3 + direction, zo)
            spread(2)
            for zo in (-3, 3, 4):
                level(zo, True)

    ix = jnp.broadcast_to(aux_ref[16:24, :][None], (8, 8, 128))
    for i in range(8):
        ix_send[i] = ix
    stage_one(0, ix_send, ix_mid, 8)

    def prepare():
        pltpu.make_async_copy(ix_recv, ix_recv, asem_r.at[0, 1]).wait()
        i, k = iota((256, 512), 0), iota((256, 512), 1)
        first = (((i >> 4) & 7) * XS + ((i >> 2) & 3)) * CS
        second = (((i >> 2) & 7) * XS + ((i >> 5) & 3)) * CS + 1
        source = jnp.where(i < 128, first, second) * 8 + (i & 3)
        names = dot(onehot(k == source), ix_recv[...].astype(BF16))
        row = names.T
        same = jnp.broadcast_to(names[:, 0:1], (256, 256)) == jnp.broadcast_to(row[0:1, :], (256, 256))
        before = same & (iota((256, 256), 1) < iota((256, 256), 0))
        order = jnp.sum(jnp.where(before, 1.0, 0.0), axis=1, keepdims=True)
        name = names[:, 0:1].astype(jnp.int32)
        at = (name >> 3) * 80 + order.astype(jnp.int32)
        spots = iota((256, 640), 1)
        tq[...] = onehot(spots == at + (name & 7) * 8)
        tv[...] = onehot(spots == at + 64)
        vmask[...] = jnp.where((iota((256, 128), 1) >> 4) == (names.astype(jnp.int32) & 7), 1.0, 0.0)
        order_row = jnp.broadcast_to(order, (256, 128)).T
        mine = (row[0:16, :].astype(jnp.int32) == me) & (order_row[0:16, :].astype(jnp.int32) == iota((16, 256), 0))
        chosen[...] = onehot(mine)

    def passing():
        return remote(hres, hin, hsem.at[0], hsem.at[1], {"segment": (seg + 1) % nseg})

    @pl.when(seg == 0)
    def _():
        hres[...] = h0_ref[...]
        hst[...] = h0_ref[...].astype(F32)

    @pl.when(seg > 0)
    def _():
        stage_two(0, ix_mid, ix_recv, 8)
        prepare()
        passing().wait_recv()
        pltpu.make_async_copy(ou_next, ou_next, nsem.at[1]).wait()
        for r in range(4):
            rows = slice(r * 64, (r + 1) * 64)
            result = (hin[rows, :].astype(F32) + dot(perm_c[rows, :], ou_next[...])).astype(BF16)
            hres[rows, :] = result
            hst[rows, :] = result.astype(F32)

    gain = gain_ref[...]
    for r in range(4):
        block = hst[r * 64:(r + 1) * 64, :]
        total = jnp.sum(jnp.sum(block * block, axis=1, keepdims=True), axis=0, keepdims=True)
        tmp[r * 64:(r + 1) * 64, :] = block * lax.rsqrt(total * (1.0 / 8192.0) + EPS) * gain

    @pl.when(seg < nseg - 1)
    def _():
        passing().start()

    def meanwhile():
        @pl.when(seg == 0)
        def _():
            stage_two(0, ix_mid, ix_recv, 8)

    gather(0, fa1, fb1, xg, meanwhile)


    for n in range(6):
        loads[n].wait()
    acc_q[...] = jnp.zeros_like(acc_q)
    acc_kv[...] = jnp.zeros_like(acc_kv)
    acc_d[...] = jnp.zeros_like(acc_d)

    def column(n):
        return pl.ds(pl.multiple_of(n * 1024, 1024), 1024)

    @pl.loop(0, 8)
    def _(n):
        acc_d[...] += dot(xg[:, column(n)], down[column(n), :])

    @pl.when(seg == 0)
    def _():
        prepare()

    low = dot(chosen[...], acc_d[...].astype(BF16)).astype(BF16)
    values = []
    for part in range(0, 8, 2):
        q_slots = [dot(low, upq[:, (part + n) * 1024:(part + n + 1) * 1024])[0:8] for n in range(2)]
        values += [dot(low, upv[:, (part + n) * 128:(part + n + 1) * 128])[0:8] for n in range(2)]
        for n in range(8):
            tile = jnp.concatenate([q[:, n * 128:(n + 1) * 128] for q in q_slots], axis=0)
            co_send[n * 80 + part * 8:n * 80 + part * 8 + 16, :] = tile.astype(BF16)
    for n, tile in enumerate(block_swap(values)):
        co_send[n * 80 + 64:n * 80 + 80, :] = tile
    in_plane(1, co_send, co_mid, 80)

    @pl.loop(0, 8)
    def _(n):
        acc_q[...] += dot(xg[:, column(n)], wq[column(n), :])

    in_plane_done(1, co_mid)
    swapped = dot(perm_s[...], co_mid[...]).astype(BF16)
    values = [co_mid[n * 80 + 64:n * 80 + 80, :].astype(F32)[0:8] for n in range(8)]
    for n, tile in enumerate(block_swap(values)):
        co_swap[n * 80:n * 80 + 64, :] = swapped[n * 64:(n + 1) * 64]
        co_swap[n * 80 + 64:n * 80 + 80, :] = tile
    along_line(1, co_swap, co_recv, 80)

    @pl.loop(0, 8)
    def _(n):
        acc_kv[...] += dot_nt(xg[:, column(n)], wkv[:, column(n)])

    along_line_done(1, co_send, co_swap, co_recv, 80)

    a, b = iota((128, 128), 0), iota((128, 128), 1)
    moved = co_recv[...]
    query = acc_q[...] + 0.5 * dot(tq[...], moved)
    narrow = onehot((b >= 16) & (b < 32) & ((a & 15) == b - 16))
    fresh = acc_kv[...] + 0.5 * dot((dot(tv[...], moved) * vmask[...]).astype(BF16), narrow)
    qk_send[...] = dot(perm_a[...], jnp.concatenate([query.astype(BF16), fresh.astype(BF16)], axis=1)).astype(BF16)
    in_plane(2, qk_send, qk_mid, 32)
    in_plane_done(2, qk_mid)
    qk_swap[...] = dot(perm_b[...], qk_mid[...]).astype(BF16)
    along_line(2, qk_swap, qk_recv, 32)
    along_line_done(2, qk_send, qk_swap, qk_recv, 32)
    rows_q[...] = dot(perm_c[...], qk_recv[...])

    loads[6].wait()
    loads[7].wait()
    spread_k = onehot(a == (b & 15))
    spread_v = onehot(a == (b & 15) + 16)
    a, b = iota((64, 128), 0), iota((64, 128), 1)
    lanes = (b >> 4) == (a & 7)
    a, b = iota((64, 64), 0), iota((64, 64), 1)
    heads = onehot((a >> 3) == (b >> 3))
    a, b = iota((64, 1024), 0), iota((64, 1024), 1)
    diagonal = (b >> 7) == (a >> 3)
    past = iota((64, 384), 1)
    scale = HD ** (-0.5)
    for r in range(4):
        cosine, sine = aux_ref[r:r + 1, :], aux_ref[4 + r:5 + r, :]
        length = aux_ref[8 + r:9 + r, 0:1].astype(jnp.int32)
        q_row = rows_q[r * 64:(r + 1) * 64, 0:128]
        kv_row = rows_q[r * 64:(r + 1) * 64, 128:256].astype(BF16)
        k_row = dot(heads, jnp.where(lanes, dot(kv_row, spread_k), 0.0).astype(BF16))
        v_row = dot(heads, jnp.where(lanes, dot(kv_row, spread_v), 0.0).astype(BF16))
        q_rot = (q_row * cosine + pltpu.roll(q_row, 64, 1) * sine).astype(BF16).astype(F32)
        k_rot = (k_row * cosine + pltpu.roll(k_row, 64, 1) * sine).astype(BF16).astype(F32)
        own = jnp.sum(q_rot * k_rot, axis=1, keepdims=True) * scale
        wide_q = jnp.where(diagonal, jnp.concatenate([q_rot] * 8, axis=1), 0.0).astype(BF16)
        scores = dot_nt(wide_q, kc[r * 384:(r + 1) * 384, :]) * scale
        valid = past < length
        scores = jnp.where(valid, scores, -1e30)
        top = jnp.maximum(jnp.max(scores, axis=1, keepdims=True), own)
        powers = jnp.where(valid, jnp.exp(scores - top), 0.0)
        own_power = jnp.exp(own - top)
        total = jnp.sum(powers, axis=1, keepdims=True) + own_power
        weights = (powers / total).astype(BF16)
        own_weight = (own_power / total).astype(BF16).astype(F32)
        mixed = dot(weights, vc[r * 384:(r + 1) * 384, :])
        mixed = jnp.concatenate([mixed[8 * g:8 * g + 8, 128 * g:128 * g + 128] for g in range(8)], axis=0)
        tmp[r * 64:(r + 1) * 64, :] = mixed + own_weight * v_row

    gather(1, fa2, fb2, ag)

    loads[8].wait()
    acc_q[...] = jnp.zeros_like(acc_q)

    @pl.loop(0, 8)
    def _(n):
        part = pl.ds(pl.multiple_of(n * 1024, 1024), 1024)
        acc_q[...] += dot(ag[:, part], wo[part, :])

    ou_send[...] = dot(perm_a[...], acc_q[...].astype(BF16)).astype(BF16)
    in_plane(3, ou_send, ou_mid, 32)
    in_plane_done(3, ou_mid)
    ou_swap[...] = dot(perm_b[...], ou_mid[...]).astype(BF16)

    @pl.when(seg < nseg - 1)
    def _():
        for k in range(8):
            other = (z + k) % 8
            remote(
                ou_swap.at[pl.ds(pl.multiple_of(other * 32, 32), 32)], ou_next.at[pl.ds(pl.multiple_of(z * 32, 32), 32)],
                nsem.at[0], nsem.at[1], {"segment": seg + 1, "wide": other * 8 + xc},
            ).start()

    along_line(3, ou_swap, ou_recv, 32)
    along_line_done(3, ou_send, ou_swap, ou_recv, 32)
    for r in range(4):
        rows = slice(r * 64, (r + 1) * 64)
        out_ref[rows, :] = (hst[rows, :] + dot(perm_c[rows, :], ou_recv[...])).astype(BF16)

    @pl.when(seg < nseg - 1)
    def _():
        passing().wait_send()
        pltpu.make_async_copy(ou_swap, ou_swap, nsem.at[0]).wait()

    for wait in pending:
        wait()
    for core in range(CS):
        @pl.when(c == core)
        def _(core=core):
            for wait in ends[core]:
                wait()


def on_device(
    entering_hidden, row_adapter_index, lengths, input_norm_gain, query_matrix, key_matrix, value_matrix,
    output_matrix, adapter_down_maps, adapter_up_query, adapter_up_value, rotated_key_cache, cached_values,
):
    half = HD // 2
    positions = lengths.reshape(4, 1).astype(F32)
    inverse = ROPE_BASE ** (-jnp.arange(half, dtype=F32) / half)
    angles = positions * inverse[None, :]
    cosine, sine = jnp.cos(angles), jnp.sin(angles)
    spread = lambda v: jnp.pad(jnp.broadcast_to(v, (4, 128)), ((0, 4), (0, 0)))
    aux = jnp.concatenate(
        [
            jnp.concatenate([cosine, cosine], 1),
            jnp.concatenate([-sine, sine], 1),
            spread(positions),
            spread(row_adapter_index.reshape(4, 1).astype(F32)),
        ],
        0,
    )
    vmem = pl.BlockSpec(memory_space=pltpu.VMEM)
    hbm = pl.BlockSpec(memory_space=pl.ANY)
    tiles = lambda rows, kind: [
        pltpu.VMEM((8, 8, rows, 128), kind), pltpu.VMEM((8, 8 * rows, 128), kind), pltpu.VMEM((64 * rows, 128), kind)
    ]
    dma = pltpu.SemaphoreType.DMA
    out = pl.pallas_call(
        kernel,
        out_shape=jax.ShapeDtypeStruct((256, 128), BF16),
        in_specs=[vmem] * 3 + [hbm] * 9,
        out_specs=vmem,
        scratch_shapes=[
            pltpu.VMEM((8192, 128), BF16), pltpu.VMEM((128, 8192), BF16), pltpu.VMEM((8192, 128), BF16),
            pltpu.VMEM((8192, 128), BF16), pltpu.VMEM((128, 8192), BF16), pltpu.VMEM((128, 1024), BF16),
            pltpu.VMEM((1536, 1024), BF16), pltpu.VMEM((1536, 1024), BF16),
            pltpu.VMEM((256, 128), F32), pltpu.VMEM((256, 128), F32),
            pltpu.VMEM((256, 128), BF16), pltpu.VMEM((256, 128), BF16),
            *[pltpu.VMEM((512, 2048), BF16)] * 4,
            pltpu.VMEM((256, 8192), BF16), pltpu.VMEM((256, 8192), BF16),
            pltpu.VMEM((256, 128), F32), pltpu.VMEM((256, 128), F32), pltpu.VMEM((256, 128), F32),
            *tiles(8, F32), *[pltpu.VMEM((640, 128), BF16)] * 4,
            *[pltpu.VMEM((256, 256), BF16)] * 4, *[pltpu.VMEM((256, 128), BF16)] * 5,
            pltpu.VMEM((256, 640), BF16), pltpu.VMEM((256, 640), BF16), pltpu.VMEM((16, 256), BF16),
            pltpu.VMEM((256, 128), F32),
            *[pltpu.VMEM((256, 256), BF16)] * 3, pltpu.VMEM((512, 640), BF16), pltpu.VMEM((256, 256), F32),
            dma((9,)), *[dma((2, 3))] * 2, *[dma((2, 2, 4, 4))] * 2, *[dma((2, 4, 9))] * 2,
            *[dma((2, 2, 4))] * 2, *[dma((2, 2, 2, 8))] * 2, *[dma((2, 5, 8))] * 2, dma((4, 2)), dma((4, 2)), dma((2,)), dma((2,)),
        ],
        compiler_params=pltpu.CompilerParams(
            collective_id=0, has_side_effects=True, vmem_limit_bytes=60 * 1024 * 1024
        ),
        name="layer_step",
    )(
        entering_hidden.reshape(256, 128),
        aux,
        input_norm_gain.astype(F32).reshape(64, 128),
        query_matrix[0],
        key_matrix[0].T,
        value_matrix[0].T,
        output_matrix[0],
        adapter_down_maps[0, 0],
        adapter_up_query[0, 0],
        adapter_up_value[0, 0],
        rotated_key_cache.reshape(1536, 1024),
        cached_values.reshape(1536, 1024),
    )
    return out.reshape(1, 2, 2, 8192)


def solution(mesh):
    placed = (
        P(None, "wide", None), P(None, "wide", None), P(None, "wide"), P("segment", None),
        P("segment", None, "wide"), P("segment", None, "wide"), P("segment", None, "wide"), P("segment", None, "wide"),
        P("segment", "wide", None, None), P("segment", "wide", None, None), P("segment", "wide", None, None),
        P("segment", None, "wide", None, None), P("segment", None, "wide", None, None),
    )
    return jax.shard_map(
        on_device, mesh=mesh, in_specs=placed, out_specs=P("segment", None, "wide", None), check_vma=False
    )
```

```python
import jax
import jax.numpy as jnp
from jax import lax
from jax.experimental import pallas as pl
from jax.experimental.pallas import tpu as pltpu
from jax.sharding import PartitionSpec as P

HD = 128
RANK = 64
EPS = 1e-05
ROPE_BASE = 500000.0
ZS, XS, CS = 8, 4, 2
MESH = pl.DeviceIdType.MESH
F32 = jnp.float32
BF16 = jnp.bfloat16


def iota(shape, dim):
    return lax.broadcasted_iota(jnp.int32, shape, dim)


def onehot(cond):
    return jnp.where(cond, 1.0, 0.0).astype(BF16)


def dot(a, b):
    return jnp.dot(a, b, preferred_element_type=F32)


def dot_nt(a, b):
    return lax.dot_general(a, b, (((1,), (1,)), ((), ())), preferred_element_type=F32)


def kernel(
    h0_ref, aux_ref, gain_ref, wq_hbm, wk_hbm, wv_hbm, wo_hbm, down_hbm, upq_hbm, upv_hbm, kc_hbm, vc_hbm,
    out_ref,
    wq, wkv, wo, down, upq, upv, kc, vc,
    hst, tmp, hin, hres,
    fa1, fa2, fb1, fb2, xg, ag, acc_q, acc_kv, acc_d,
    ix_send, ix_mid, ix_recv, co_send, co_mid, co_swap, co_recv, qk_send, qk_mid, qk_swap, qk_recv, ou_send, ou_mid, ou_swap, ou_recv, ou_next,
    tq, tv, chosen, vmask, perm_a, perm_b, perm_c, perm_s, rows_q,
    wsem, xa_s, xa_r, za_s, za_r, ua_s, ua_r, zb_s, zb_r, xb_s, xb_r, ub_s, ub_r, asem_s, asem_r, hsem, nsem,
):
    seg = lax.axis_index("segment")
    me = lax.axis_index("wide")
    nseg = lax.axis_size("segment")
    z = me // (XS * CS)
    xc = me % (XS * CS)
    x = xc // CS
    c = xc % CS
    grp = z * CS + c

    def wide(zz, xx, cc):
        return {"wide": (zz * XS + xx) * CS + cc}

    def remote(src, dst, ssem, rsem, dev):
        return pltpu.make_async_remote_copy(
            src_ref=src, dst_ref=dst, send_sem=ssem, recv_sem=rsem, device_id=dev, device_id_type=MESH
        )

    loads = [
        pltpu.make_async_copy(wq_hbm, wq, wsem.at[0]),
        pltpu.make_async_copy(wk_hbm, wkv.at[pl.ds(0, 16)], wsem.at[1]),
        pltpu.make_async_copy(wv_hbm, wkv.at[pl.ds(16, 16)], wsem.at[2]),
        pltpu.make_async_copy(down_hbm, down, wsem.at[3]),
        pltpu.make_async_copy(upq_hbm, upq.at[pl.ds(0, RANK)], wsem.at[4]),
        pltpu.make_async_copy(upv_hbm, upv.at[pl.ds(RANK, RANK)], wsem.at[5]),
        pltpu.make_async_copy(kc_hbm, kc, wsem.at[6]),
        pltpu.make_async_copy(vc_hbm, vc, wsem.at[7]),
        pltpu.make_async_copy(wo_hbm, wo, wsem.at[8]),
    ]
    for load in loads:
        load.start()

    barrier = pltpu.get_barrier_semaphore()
    for k in range(1, 8):
        other = (xc + k) % 8
        pl.semaphore_signal(barrier, inc=1, device_id={"wide": z * 8 + other}, device_id_type=MESH)
        pl.semaphore_signal(barrier, inc=1, device_id={"wide": ((z + k) % 8) * 8 + xc}, device_id_type=MESH)

    for k in (1, nseg - 1):
        for other in range(8):
            pl.semaphore_signal(
                barrier, inc=1, device_id={"segment": (seg + k) % nseg, "wide": other * 8 + xc}, device_id_type=MESH
            )
    wkv[32:128, :] = jnp.zeros((96, wkv.shape[1]), BF16)
    upq[RANK:2 * RANK, :] = jnp.zeros((RANK, upq.shape[1]), BF16)
    upv[0:RANK, :] = jnp.zeros((RANK, upv.shape[1]), BF16)
    i, k = iota((256, 256), 0), iota((256, 256), 1)
    zi, xi, ri = (i >> 2) & 7, i >> 6, i & 3
    perm_a[...] = onehot(k == jnp.where((i & 32) == 0, zi * 16 + xi * 4, 128 + xi * 32 + zi * 4) + ri)
    perm_b[...] = onehot(k == zi * 32 + (i >> 5) * 4 + ri)
    perm_c[...] = onehot(k == (i & 63) * 4 + (i >> 6))
    i, k = iota((512, 640), 0), iota((512, 640), 1)
    perm_s[...] = onehot(k == ((i >> 3) & 7) * 80 + (i >> 6) * 8 + (i & 7))
    gain = gain_ref[...].astype(F32).reshape(64, 128)
    for m in range(2):
        pair = h0_ref[m].astype(F32)
        for n in range(2):
            hst[(2 * m + n) * 64:(2 * m + n + 1) * 64, :] = pair[n:n + 1].reshape(64, 128)
    pl.semaphore_wait(barrier, 30)

    pending = []

    def stage_one(number, send, mid, rows):
        dest = mid.at[:, pl.ds(pl.multiple_of(xc * rows, rows), rows), :]
        pltpu.make_async_copy(send.at[xc], dest, asem_r.at[number, 0]).start()
        for k in (4, 3, 5, 2, 6, 1, 7):
            other = (xc + k) % 8
            remote(send.at[other], dest, asem_s.at[number, 0], asem_r.at[number, 0], {"wide": z * 8 + other}).start()

    def stage_two(number, mid, recv, rows):
        pltpu.make_async_copy(mid, mid, asem_r.at[number, 0]).wait()
        mine = pl.ds(pl.multiple_of(z * 8 * rows, 8 * rows), 8 * rows)
        pltpu.make_async_copy(mid.at[z], recv.at[mine], asem_r.at[number, 1]).start()
        for k in (4, 3, 5, 2, 6, 1, 7):
            other = (z + k) % 8
            remote(
                mid.at[other], recv.at[mine], asem_s.at[number, 1], asem_r.at[number, 1], {"wide": other * 8 + xc}
            ).start()

    for side, ref in enumerate((ix_send, ix_mid)):
        pending.append(
            lambda side=side, ref=ref: pltpu.make_async_copy(ref.at[pl.ds(0, 7)], ref.at[pl.ds(0, 7)], asem_s.at[0, side]).wait()
        )

    def in_plane(number, send, mid, count):
        def rows(n):
            return pl.ds(pl.multiple_of(n * count, 16), count)

        pltpu.make_async_copy(send.at[rows(xc)], mid.at[rows(xc)], asem_r.at[number, 0]).start()
        for k in (4, 3, 5, 2, 6, 1, 7):
            other = (xc + k) % 8
            remote(
                send.at[rows(other)], mid.at[rows(xc)], asem_s.at[number, 0], asem_r.at[number, 0], {"wide": z * 8 + other}
            ).start()

    def in_plane_done(number, mid):
        pltpu.make_async_copy(mid, mid, asem_r.at[number, 0]).wait()

    def along_line(number, swapped, recv, count):
        def rows(n):
            return pl.ds(pl.multiple_of(n * count, 16), count)

        pltpu.make_async_copy(swapped.at[rows(z)], recv.at[rows(z)], asem_r.at[number, 1]).start()
        for k in (4, 3, 5, 2, 6, 1, 7):
            other = (z + k) % 8
            remote(
                swapped.at[rows(other)], recv.at[rows(z)], asem_s.at[number, 1], asem_r.at[number, 1], {"wide": other * 8 + xc}
            ).start()

    def along_line_done(number, send, swapped, recv, count):
        pltpu.make_async_copy(recv, recv, asem_r.at[number, 1]).wait()
        part = pl.ds(0, 7 * count)
        pending.append(lambda: pltpu.make_async_copy(send.at[part], send.at[part], asem_s.at[number, 0]).wait())
        pending.append(lambda: pltpu.make_async_copy(swapped.at[part], swapped.at[part], asem_s.at[number, 1]).wait())

    def block_swap(tiles):
        block = iota((8, 128), 1) >> 4
        shifted = [[pltpu.roll(t, 16 * k, 1) if k else t for t in tiles] for k in range(8)]
        swapped = []
        for p in range(8):
            total = jnp.zeros((8, 128), F32)
            for k in range(8):
                total = jnp.where(block == (p + k) % 8, shifted[k][(p + k) % 8], total)
            swapped.append(jnp.concatenate([total, jnp.zeros((8, 128), F32)], axis=0).astype(BF16))
        return swapped

    def fold(dest, base):
        for m in range(16):
            dest[pl.ds(base, 16), m * 128:(m + 1) * 128] = tmp[pl.ds(m, 16, stride=16), :].astype(BF16)

    def unfold(source, base, dest, to):
        i, k = iota((64, 64), 0), iota((64, 64), 1)
        perm = onehot(k == ((i >> 2) & 3) * 16 + (i & 3) * 4 + (i >> 4))
        for part in range(4):
            moved = dot(perm, source[pl.ds(base, 64), part * 512:(part + 1) * 512]).astype(BF16)
            for q in range(4):
                dest[pl.ds(to, 16), q * 2048 + part * 512:q * 2048 + (part + 1) * 512] = moved[16 * q:16 * q + 16]

    ends = {0: [], 1: []}

    def gather(number, fa, fb, full, meanwhile=lambda: None):
        partner = wide(z, x, 1 - c)

        def block(xo, zo, half=None):
            at = pl.multiple_of((((x + xo) % XS) * ZS + (z + zo) % ZS) * 16, 16)
            return fb.at[pl.ds(at, 16), pl.ds(0, 2048) if half is None else pl.ds(half * 1024, 1024)]

        def block_a(xo, zo, half=None):
            at = pl.multiple_of((((z + zo) % ZS) * XS + (x + xo) % XS) * 16, 16)
            return fa.at[pl.ds(at, 16), pl.ds(0, 2048) if half is None else pl.ds(half * 1024, 1024)]

        def share_a(xo, zo, half=None):
            s = number, xo, 8 if half == 1 else zo % ZS
            at = block_a(xo, zo, half)
            return remote(at, at, ua_s.at[s], ua_r.at[s], partner)

        def share_b(kind, zo):
            s = number, kind, zo % ZS
            at = block((0, 3, 1, 2, 2)[kind], zo, (None, None, None, 0, 1)[kind])
            return remote(at, at, ub_s.at[s], ub_r.at[s], partner)

        def spread(xo):
            for zh in range(2):
                xx = (x + xo) % XS
                unfold(
                    fb, pl.multiple_of((xx * ZS + zh * 4) * 16, 64), full, pl.multiple_of(128 + xx * 32 + zh * 16, 16)
                )

        def level(zo, wait):
            if wait:
                for xo in range(XS):
                    for half in (0, 1) if zo == 4 else (None,):
                        share_a(xo, zo, half).wait_recv()
            zz = (z + zo) % ZS
            unfold(fa, pl.multiple_of(zz * 64, 64), full, pl.multiple_of(zz * 16, 16))

        @pl.when(c == 0)
        def _():
            sent = ends[0]

            def go(make, *args):
                make(*args).start()
                sent.append(lambda: make(*args).wait_send())

            def hop(k, offset=0):
                at = block_a(offset, 0)
                return remote(at, at, xa_s.at[number, k - 1], xa_r.at[number, k - 1], wide(z, (x + k) % XS, c))

            def ring(direction, step, xo, half=None):
                at = block_a(xo, -step if direction == 0 else step, half)
                s = number, direction, step, xo
                target = (z + (1 if direction == 0 else ZS - 1)) % ZS
                return remote(at, at, za_s.at[s], za_r.at[s], wide(target, x, c))

            def landed(direction, step, xo, half=None):
                at = block_a(xo, -(step + 1) if direction == 0 else step + 1, half)
                s = number, direction, step, xo
                remote(at, at, za_s.at[s], za_r.at[s], partner).wait_recv()

            def enter(xo):
                go(ring, 0, 0, xo)
                go(ring, 1, 0, xo)
                go(share_a, xo, 0)

            def onward(step, xo):
                for direction in range(2):
                    landed(direction, step, xo)
                    go(ring, direction, step + 1, xo, None if step < 2 else direction)
                    go(share_a, xo, -(step + 1) if direction == 0 else step + 1)

            fold(fa, pl.multiple_of((z * XS + x) * 16, 16))
            for k in (2, 1, 3):
                go(hop, k)
            enter(0)
            for k in (1, 3):
                hop(k, XS - k).wait_recv()
                enter(XS - k)
            onward(0, 0)
            hop(2, 2).wait_recv()
            enter(2)
            level(0, False)
            for xo in (3, 1, 2):
                onward(0, xo)
            meanwhile()
            for step in (1, 2):
                level(-step, False)
                level(step, False)
                for xo in (0, 3, 1, 2):
                    onward(step, xo)
            level(-3, False)
            level(3, False)
            for kinds, xo in (((0,), 0), ((1,), 3), ((2,), 1), ((3, 4), 2)):
                if xo == 2:
                    for xq in (0, 3, 1, 2):
                        for direction in range(2):
                            landed(direction, 3, xq, direction)
                            go(share_a, xq, 4, direction)
                    level(4, False)
                for zo in range(ZS):
                    for kind in kinds:
                        share_b(kind, zo).wait_recv()
                spread(xo)

        @pl.when(c == 1)
        def _():
            sent = ends[1]

            def go(make, *args):
                make(*args).start()
                sent.append(lambda: make(*args).wait_send())

            def along_z(direction, step, half=None):
                at = block(0, -step if direction == 0 else step, half)
                s = number, direction, step
                target = (z + (1 if direction == 0 else ZS - 1)) % ZS
                return remote(at, at, zb_s.at[s], zb_r.at[s], wide(target, x, c))

            def from_z(direction, step, half=None):
                at = block(0, -(step + 1) if direction == 0 else step + 1, half)
                s = number, direction, step
                remote(at, at, zb_s.at[s], zb_r.at[s], partner).wait_recv()

            def along_x(direction, step, zo):
                at = block(0, zo) if step == 0 else block(3 if direction == 0 else 1, zo, direction)
                s = number, direction, step, zo % ZS
                target = (x + (1 if direction == 0 else XS - 1)) % XS
                return remote(at, at, xb_s.at[s], xb_r.at[s], wide(z, target, c))

            def from_x(direction, step, zo):
                at = block(3 if direction == 0 else 1, zo) if step == 0 else block(2, zo, direction)
                s = number, direction, step, zo % ZS
                remote(at, at, xb_s.at[s], xb_r.at[s], partner).wait_recv()

            def have(zo):
                go(along_x, 0, 0, zo)
                go(along_x, 1, 0, zo)
                go(share_b, 0, zo)

            def relay(zo):
                for direction in range(2):
                    from_x(direction, 0, zo)
                    go(along_x, direction, 1, zo)
                    go(share_b, 1 + direction, zo)

            fold(fb, pl.multiple_of((x * ZS + z) * 16, 16))
            go(along_z, 0, 0)
            go(along_z, 1, 0)
            have(0)
            for step in range(3):
                for direction in range(2):
                    from_z(direction, step)
                    go(along_z, direction, step + 1, None if step < 2 else direction)
                    have(-(step + 1) if direction == 0 else step + 1)
                if step == 0:
                    relay(0)
                    meanwhile()
                else:
                    relay(-step)
                    relay(step)
            from_z(0, 3, 0)
            from_z(1, 3, 1)
            have(4)
            relay(-3)
            relay(3)
            level(0, True)
            spread(0)
            relay(4)
            level(-1, True)
            level(1, True)
            spread(3)
            spread(1)
            level(-2, True)
            level(2, True)
            for zo in (0, 7, 1, 6, 2, 5, 3, 4):
                for direction in range(2):
                    from_x(direction, 1, zo)
                    go(share_b, 3 + direction, zo)
            spread(2)
            for zo in (-3, 3, 4):
                level(zo, True)

    ix = jnp.broadcast_to(aux_ref[16:24, :][None], (8, 8, 128))
    for i in range(8):
        ix_send[i] = ix
    stage_one(0, ix_send, ix_mid, 8)

    def prepare():
        pltpu.make_async_copy(ix_recv, ix_recv, asem_r.at[0, 1]).wait()
        i, k = iota((256, 512), 0), iota((256, 512), 1)
        first = (((i >> 4) & 7) * XS + ((i >> 2) & 3)) * CS
        second = (((i >> 2) & 7) * XS + ((i >> 5) & 3)) * CS + 1
        source = jnp.where(i < 128, first, second) * 8 + (i & 3)
        names = dot(onehot(k == source), ix_recv[...].astype(BF16))
        row = names.T
        same = jnp.broadcast_to(names[:, 0:1], (256, 256)) == jnp.broadcast_to(row[0:1, :], (256, 256))
        before = same & (iota((256, 256), 1) < iota((256, 256), 0))
        order = jnp.sum(jnp.where(before, 1.0, 0.0), axis=1, keepdims=True)
        name = names[:, 0:1].astype(jnp.int32)
        at = (name >> 3) * 80 + order.astype(jnp.int32)
        spots = iota((256, 640), 1)
        tq[...] = onehot(spots == at + (name & 7) * 8)
        tv[...] = onehot(spots == at + 64)
        vmask[...] = jnp.where((iota((256, 128), 1) >> 4) == (names.astype(jnp.int32) & 7), 1.0, 0.0)
        order_row = jnp.broadcast_to(order, (256, 128)).T
        mine = (row[0:16, :].astype(jnp.int32) == me) & (order_row[0:16, :].astype(jnp.int32) == iota((16, 256), 0))
        chosen[...] = onehot(mine)

    def passing():
        return remote(hres, hin, hsem.at[0], hsem.at[1], {"segment": (seg + 1) % nseg})

    @pl.when(seg == 0)
    def _():
        hres[...] = hst[...].astype(BF16)

    @pl.when(seg > 0)
    def _():
        stage_two(0, ix_mid, ix_recv, 8)
        prepare()
        passing().wait_recv()
        pltpu.make_async_copy(ou_next, ou_next, nsem.at[1]).wait()
        for r in range(4):
            rows = slice(r * 64, (r + 1) * 64)
            result = (hin[rows, :].astype(F32) + dot(perm_c[rows, :], ou_next[...])).astype(BF16)
            hres[rows, :] = result
            hst[rows, :] = result.astype(F32)

    for r in range(4):
        block = hst[r * 64:(r + 1) * 64, :]
        total = jnp.sum(jnp.sum(block * block, axis=1, keepdims=True), axis=0, keepdims=True)
        tmp[r * 64:(r + 1) * 64, :] = block * lax.rsqrt(total * (1.0 / 8192.0) + EPS) * gain

    @pl.when(seg < nseg - 1)
    def _():
        passing().start()

    def meanwhile():
        @pl.when(seg == 0)
        def _():
            stage_two(0, ix_mid, ix_recv, 8)

    gather(0, fa1, fb1, xg, meanwhile)


    for n in range(6):
        loads[n].wait()
    acc_q[...] = jnp.zeros_like(acc_q)
    acc_kv[...] = jnp.zeros_like(acc_kv)
    acc_d[...] = jnp.zeros_like(acc_d)

    def column(n):
        return pl.ds(pl.multiple_of(n * 1024, 1024), 1024)

    @pl.loop(0, 8)
    def _(n):
        acc_d[...] += dot(xg[:, column(n)], down[column(n), :])

    @pl.when(seg == 0)
    def _():
        prepare()

    low = dot(chosen[...], acc_d[...].astype(BF16)).astype(BF16)
    values = []
    for part in range(0, 8, 2):
        q_slots = [dot(low, upq[:, (part + n) * 1024:(part + n + 1) * 1024])[0:8] for n in range(2)]
        values += [dot(low, upv[:, (part + n) * 128:(part + n + 1) * 128])[0:8] for n in range(2)]
        for n in range(8):
            tile = jnp.concatenate([q[:, n * 128:(n + 1) * 128] for q in q_slots], axis=0)
            co_send[n * 80 + part * 8:n * 80 + part * 8 + 16, :] = tile.astype(BF16)
    for n, tile in enumerate(block_swap(values)):
        co_send[n * 80 + 64:n * 80 + 80, :] = tile
    in_plane(1, co_send, co_mid, 80)

    @pl.loop(0, 8)
    def _(n):
        acc_q[...] += dot(xg[:, column(n)], wq[column(n), :])

    in_plane_done(1, co_mid)
    swapped = dot(perm_s[...], co_mid[...]).astype(BF16)
    values = [co_mid[n * 80 + 64:n * 80 + 80, :].astype(F32)[0:8] for n in range(8)]
    for n, tile in enumerate(block_swap(values)):
        co_swap[n * 80:n * 80 + 64, :] = swapped[n * 64:(n + 1) * 64]
        co_swap[n * 80 + 64:n * 80 + 80, :] = tile
    along_line(1, co_swap, co_recv, 80)

    @pl.loop(0, 8)
    def _(n):
        acc_kv[...] += dot_nt(xg[:, column(n)], wkv[:, column(n)])

    along_line_done(1, co_send, co_swap, co_recv, 80)

    a, b = iota((128, 128), 0), iota((128, 128), 1)
    moved = co_recv[...]
    query = acc_q[...] + 0.5 * dot(tq[...], moved)
    narrow = onehot((b >= 16) & (b < 32) & ((a & 15) == b - 16))
    fresh = acc_kv[...] + 0.5 * dot((dot(tv[...], moved) * vmask[...]).astype(BF16), narrow)
    qk_send[...] = dot(perm_a[...], jnp.concatenate([query.astype(BF16), fresh.astype(BF16)], axis=1)).astype(BF16)
    in_plane(2, qk_send, qk_mid, 32)
    in_plane_done(2, qk_mid)
    qk_swap[...] = dot(perm_b[...], qk_mid[...]).astype(BF16)
    along_line(2, qk_swap, qk_recv, 32)
    along_line_done(2, qk_send, qk_swap, qk_recv, 32)
    rows_q[...] = dot(perm_c[...], qk_recv[...])

    loads[6].wait()
    loads[7].wait()
    spread_k = onehot(a == (b & 15))
    spread_v = onehot(a == (b & 15) + 16)
    a, b = iota((64, 128), 0), iota((64, 128), 1)
    lanes = (b >> 4) == (a & 7)
    a, b = iota((64, 64), 0), iota((64, 64), 1)
    heads = onehot((a >> 3) == (b >> 3))
    a, b = iota((64, 1024), 0), iota((64, 1024), 1)
    diagonal = (b >> 7) == (a >> 3)
    past = iota((64, 384), 1)
    scale = HD ** (-0.5)
    for r in range(4):
        cosine, sine = aux_ref[r:r + 1, :], aux_ref[4 + r:5 + r, :]
        length = aux_ref[8 + r:9 + r, 0:1].astype(jnp.int32)
        q_row = rows_q[r * 64:(r + 1) * 64, 0:128]
        kv_row = rows_q[r * 64:(r + 1) * 64, 128:256].astype(BF16)
        k_row = dot(heads, jnp.where(lanes, dot(kv_row, spread_k), 0.0).astype(BF16))
        v_row = dot(heads, jnp.where(lanes, dot(kv_row, spread_v), 0.0).astype(BF16))
        q_rot = (q_row * cosine + pltpu.roll(q_row, 64, 1) * sine).astype(BF16).astype(F32)
        k_rot = (k_row * cosine + pltpu.roll(k_row, 64, 1) * sine).astype(BF16).astype(F32)
        own = jnp.sum(q_rot * k_rot, axis=1, keepdims=True) * scale
        wide_q = jnp.where(diagonal, jnp.concatenate([q_rot] * 8, axis=1), 0.0).astype(BF16)
        scores = dot_nt(wide_q, kc[r * 384:(r + 1) * 384, :]) * scale
        valid = past < length
        scores = jnp.where(valid, scores, -1e30)
        top = jnp.maximum(jnp.max(scores, axis=1, keepdims=True), own)
        powers = jnp.where(valid, jnp.exp(scores - top), 0.0)
        own_power = jnp.exp(own - top)
        total = jnp.sum(powers, axis=1, keepdims=True) + own_power
        weights = (powers / total).astype(BF16)
        own_weight = (own_power / total).astype(BF16).astype(F32)
        mixed = dot(weights, vc[r * 384:(r + 1) * 384, :])
        mixed = jnp.concatenate([mixed[8 * g:8 * g + 8, 128 * g:128 * g + 128] for g in range(8)], axis=0)
        tmp[r * 64:(r + 1) * 64, :] = mixed + own_weight * v_row

    gather(1, fa2, fb2, ag)

    loads[8].wait()
    acc_q[...] = jnp.zeros_like(acc_q)

    @pl.loop(0, 8)
    def _(n):
        part = pl.ds(pl.multiple_of(n * 1024, 1024), 1024)
        acc_q[...] += dot(ag[:, part], wo[part, :])

    ou_send[...] = dot(perm_a[...], acc_q[...].astype(BF16)).astype(BF16)
    in_plane(3, ou_send, ou_mid, 32)
    in_plane_done(3, ou_mid)
    ou_swap[...] = dot(perm_b[...], ou_mid[...]).astype(BF16)

    @pl.when(seg < nseg - 1)
    def _():
        for k in (4, 3, 5, 2, 6, 1, 7, 0):
            other = (z + k) % 8
            remote(
                ou_swap.at[pl.ds(pl.multiple_of(other * 32, 32), 32)], ou_next.at[pl.ds(pl.multiple_of(z * 32, 32), 32)],
                nsem.at[0], nsem.at[1], {"segment": seg + 1, "wide": other * 8 + xc},
            ).start()

    along_line(3, ou_swap, ou_recv, 32)
    along_line_done(3, ou_send, ou_swap, ou_recv, 32)
    for r in range(4):
        rows = slice(r * 64, (r + 1) * 64)
        out_ref[rows, :] = (hst[rows, :] + dot(perm_c[rows, :], ou_recv[...])).astype(BF16)

    @pl.when(seg < nseg - 1)
    def _():
        passing().wait_send()
        pltpu.make_async_copy(ou_swap, ou_swap, nsem.at[0]).wait()

    for wait in pending:
        wait()
    for core in range(CS):
        @pl.when(c == core)
        def _(core=core):
            for wait in ends[core]:
                wait()


def on_device(
    entering_hidden, row_adapter_index, lengths, input_norm_gain, query_matrix, key_matrix, value_matrix,
    output_matrix, adapter_down_maps, adapter_up_query, adapter_up_value, rotated_key_cache, cached_values,
):
    half = HD // 2
    positions = lengths.reshape(4, 1).astype(F32)
    inverse = ROPE_BASE ** (-jnp.arange(half, dtype=F32) / half)
    angles = positions * inverse[None, :]
    cosine, sine = jnp.cos(angles), jnp.sin(angles)
    spread = lambda v: jnp.pad(jnp.broadcast_to(v, (4, 128)), ((0, 4), (0, 0)))
    aux = jnp.concatenate(
        [
            jnp.concatenate([cosine, cosine], 1),
            jnp.concatenate([-sine, sine], 1),
            spread(positions),
            spread(row_adapter_index.reshape(4, 1).astype(F32)),
        ],
        0,
    )
    vmem = pl.BlockSpec(memory_space=pltpu.VMEM)
    hbm = pl.BlockSpec(memory_space=pl.ANY)
    tiles = lambda rows, kind: [
        pltpu.VMEM((8, 8, rows, 128), kind), pltpu.VMEM((8, 8 * rows, 128), kind), pltpu.VMEM((64 * rows, 128), kind)
    ]
    dma = pltpu.SemaphoreType.DMA
    out = pl.pallas_call(
        kernel,
        out_shape=jax.ShapeDtypeStruct((256, 128), BF16),
        in_specs=[vmem] * 3 + [hbm] * 9,
        out_specs=vmem,
        scratch_shapes=[
            pltpu.VMEM((8192, 128), BF16), pltpu.VMEM((128, 8192), BF16), pltpu.VMEM((8192, 128), BF16),
            pltpu.VMEM((8192, 128), BF16), pltpu.VMEM((128, 8192), BF16), pltpu.VMEM((128, 1024), BF16),
            pltpu.VMEM((1536, 1024), BF16), pltpu.VMEM((1536, 1024), BF16),
            pltpu.VMEM((256, 128), F32), pltpu.VMEM((256, 128), F32),
            pltpu.VMEM((256, 128), BF16), pltpu.VMEM((256, 128), BF16),
            *[pltpu.VMEM((512, 2048), BF16)] * 4,
            pltpu.VMEM((256, 8192), BF16), pltpu.VMEM((256, 8192), BF16),
            pltpu.VMEM((256, 128), F32), pltpu.VMEM((256, 128), F32), pltpu.VMEM((256, 128), F32),
            *tiles(8, F32), *[pltpu.VMEM((640, 128), BF16)] * 4,
            *[pltpu.VMEM((256, 256), BF16)] * 4, *[pltpu.VMEM((256, 128), BF16)] * 5,
            pltpu.VMEM((256, 640), BF16), pltpu.VMEM((256, 640), BF16), pltpu.VMEM((16, 256), BF16),
            pltpu.VMEM((256, 128), F32),
            *[pltpu.VMEM((256, 256), BF16)] * 3, pltpu.VMEM((512, 640), BF16), pltpu.VMEM((256, 256), F32),
            dma((9,)), *[dma((2, 3))] * 2, *[dma((2, 2, 4, 4))] * 2, *[dma((2, 4, 9))] * 2,
            *[dma((2, 2, 4))] * 2, *[dma((2, 2, 2, 8))] * 2, *[dma((2, 5, 8))] * 2, dma((4, 2)), dma((4, 2)), dma((2,)), dma((2,)),
        ],
        compiler_params=pltpu.CompilerParams(
            collective_id=0, has_side_effects=True, vmem_limit_bytes=60 * 1024 * 1024
        ),
        name="layer_step",
    )(
        entering_hidden,
        aux,
        input_norm_gain,
        query_matrix[0],
        key_matrix[0].T,
        value_matrix[0].T,
        output_matrix[0],
        adapter_down_maps[0, 0],
        adapter_up_query[0, 0],
        adapter_up_value[0, 0],
        rotated_key_cache.reshape(1536, 1024),
        cached_values.reshape(1536, 1024),
    )
    return out.reshape(1, 2, 2, 8192)


def solution(mesh):
    placed = (
        P(None, "wide", None), P(None, "wide", None), P(None, "wide"), P("segment", None),
        P("segment", None, "wide"), P("segment", None, "wide"), P("segment", None, "wide"), P("segment", None, "wide"),
        P("segment", "wide", None, None), P("segment", "wide", None, None), P("segment", "wide", None, None),
        P("segment", None, "wide", None, None), P("segment", None, "wide", None, None),
    )
    return jax.shard_map(
        on_device, mesh=mesh, in_specs=placed, out_specs=P("segment", None, "wide", None), check_vma=False
    )
```
